512 devices in a mesh: shot: 16 (over y, core), brick: 32 (over x, z).
Axes of the slice: x: 4, y: 8, z: 8, core: 2. Of those that a mesh axis runs over, the one named last changes fastest.
Arguments:
- pressure: float32 [128, 1024, 512], P('shot', 'brick'), may hold values from -6 to 6
- auxiliary: float32 [128, 1024, 512], P('shot', 'brick'), may hold values from -6 to 6
- pressure_prior: float32 [128, 1024, 512], P('shot', 'brick'), may hold values from -6 to 6
- auxiliary_prior: float32 [128, 1024, 512], P('shot', 'brick'), may hold values from -6 to 6
- courant_sq: float32 [1024, 512], P('brick'), may hold values from 0.05 to 0.2
- thomsen_epsilon: float32 [1024, 512], P('brick'), may hold values from 0.1 to 0.35
- thomsen_delta: float32 [1024, 512], P('brick'), may hold values from 0 to 0.1
- tilt_angle: float32 [1024, 512], P('brick'), may hold values from -3.140625 to 3.140625
- frequencies: float32 [16], replicated, may hold values from 0.05 to 1.5
- spectra: float32 [128, 32, 16384], P('shot', None, 'brick'), may hold values from -6 to 6
- target_cells: int32 [16384], P('brick'), may hold values from 0 to 16383, as said below
- patch_lists: int32 [32, 16, 3, 128], P('brick'), may hold values from 0 to 511, as said below
- patch_counts: int32 [32, 16], P('brick', 'shot'), may hold values from 1 to 3, as said below
Outputs:
- pressure_out: float32 [128, 1024, 512], P('shot', 'brick')
- auxiliary_out: float32 [128, 1024, 512], P('shot', 'brick')
- spectra_out: float32 [128, 32, 16384], P('shot', None, 'brick')
- gram_tiles: float32 [32, 16, 3, 128, 128], P('brick', 'shot')
The draws below stay inside these ranges and needn't reach their ends.
Inputs may be any that keep to these rules, and one draw needn't show every extreme that they name: `target_cells`: the block of each brick holds distinct cells of that brick. `patch_lists`: target numbers within the owner's brick; the cells of one patch slot are distinct. `patch_counts`: in every brick some owner has all 3 slots live.
All inputs are finite; a program needn't handle non-finite values.
Results may differ from the reference program's by a relative error of at most 0.00077.
Values may be sent and summed in bfloat16 or wider, within the bound.
A program may use at most 64 MiB of HBM per device.

```python
import math
import jax
import jax.numpy as jnp
from jax import lax

CX = 32
CZ = 512
STEPS = 4
FREQ = 16
TGT_BRICK = 512
PATCH = 128
P_MAX = 3
GROUPS = 16
BRICKS = 32
NX = 1024
SHOTS = 128
TARGETS = 16384
FEATURES = 4096


def draw_target_cells(key, part):
    keys = jax.random.split(jax.random.fold_in(key, 11), BRICKS)
    chosen = jax.vmap(lambda single: jax.random.permutation(single, CX * CZ)[:TGT_BRICK])(keys)
    return chosen.reshape(-1).astype(jnp.int32)


def draw_patch_lists(key, part):
    keys = jax.random.split(jax.random.fold_in(key, 23), BRICKS * GROUPS * P_MAX)
    chosen = jax.vmap(lambda single: jax.random.permutation(single, TGT_BRICK)[:PATCH])(keys)
    return chosen.reshape(BRICKS, GROUPS, P_MAX, PATCH).astype(jnp.int32)


def draw_patch_counts(key, part):
    first, second = jax.random.split(jax.random.fold_in(key, 37))
    counts = jax.random.randint(first, (BRICKS, GROUPS), 1, P_MAX + 1)
    fullest = jax.random.randint(second, (BRICKS,), 0, GROUPS)
    places = jnp.arange(GROUPS)[None, :] == fullest[:, None]
    return jnp.where(places, P_MAX, counts).astype(jnp.int32)


def shard_levels(key, extent, pieces, low, top_value):
    loudness = 1.0
    for position, parts in pieces:
        draws = jax.random.uniform(jax.random.fold_in(jax.random.fold_in(key, 6), position), (parts,), jnp.float32, low / len(pieces), top_value / len(pieces))
        loudness = loudness * jnp.repeat(jnp.exp(draws), extent[position] // parts).reshape((-1,) + (1,) * (len(extent) - 1 - position))
    return loudness


def gaussian(rng, dims, spread, most, cuts=(), kind=jnp.bfloat16):
    values = jax.random.normal(rng, dims, jnp.float32) * spread
    if len(cuts) > 0:
        values = shard_levels(rng, dims, cuts, -0.22, 0.18) * values
    return jnp.clip(values, min=-most, max=most).astype(kind)


def setup_inputs(seed: int = 0) -> dict:
    seeds = jax.random.split(jax.random.key(seed), 14)
    return {
        "pressure": gaussian(seeds[0], (SHOTS, NX, CZ), 1.0, 6.0, ((0, 16), (1, 32)), jnp.float32),
        "auxiliary": gaussian(seeds[1], (SHOTS, NX, CZ), 1.0, 6.0, ((0, 16), (1, 32)), jnp.float32),
        "pressure_prior": gaussian(seeds[2], (SHOTS, NX, CZ), 1.0, 6.0, ((0, 16), (1, 32)), jnp.float32),
        "auxiliary_prior": gaussian(seeds[3], (SHOTS, NX, CZ), 1.0, 6.0, ((0, 16), (1, 32)), jnp.float32),
        "courant_sq": jnp.clip(jnp.exp(math.log(0.2) - 1.3862944 * jax.random.uniform(seeds[4], (NX, CZ), jnp.float32) ** shard_levels(seeds[4], (NX, CZ), ((0, 32),), -0.2, 0.2)), 0.05, 0.2),
        "thomsen_epsilon": jnp.clip(0.1 + 0.25 * jax.random.uniform(seeds[5], (NX, CZ), jnp.float32) ** shard_levels(seeds[5], (NX, CZ), ((0, 32),), -0.2, 0.2), 0.1, 0.35),
        "thomsen_delta": jnp.clip(0.1 * jax.random.uniform(seeds[6], (NX, CZ), jnp.float32) ** shard_levels(seeds[6], (NX, CZ), ((0, 32),), -0.2, 0.2), 0.0, 0.1),
        "tilt_angle": jnp.clip(jax.random.uniform(seeds[7], (NX, CZ), jnp.float32, -3.140625, 3.140625), -3.140625, 3.140625),
        "frequencies": jnp.clip(jnp.exp(jax.random.uniform(seeds[8], (FREQ,), jnp.float32, math.log(0.05), math.log(1.5))), 0.05, 1.5),
        "spectra": gaussian(seeds[9], (SHOTS, 2 * FREQ, TARGETS), 1.0, 6.0, ((0, 16), (2, 32)), jnp.float32),
        "target_cells": draw_target_cells(jax.random.fold_in(seeds[13], 71), 0),
        "patch_lists": draw_patch_lists(jax.random.fold_in(seeds[13], 71), 0),
        "patch_counts": draw_patch_counts(jax.random.fold_in(seeds[13], 71), 0),
    }


def tilt_terms(tilt_angle):
    sine = jnp.sin(tilt_angle)
    cosine = jnp.cos(tilt_angle)
    return sine * sine, cosine * cosine, 2.0 * sine * cosine


def derivatives(field, sine_sq, cosine_sq, double_sin):
    widths = [(0, 0)] * (field.ndim - 1) + [(1, 1)]
    padded = jnp.pad(field, widths)
    centre = padded[..., 1:-1, 1:-1]
    second_x = padded[..., 2:, 1:-1] - 2.0 * centre + padded[..., :-2, 1:-1]
    second_z = padded[..., 1:-1, 2:] - 2.0 * centre + padded[..., 1:-1, :-2]
    mixed = 0.25 * (padded[..., 2:, 2:] - padded[..., 2:, :-2] - padded[..., :-2, 2:] + padded[..., :-2, :-2])
    along_axis = sine_sq * second_x + cosine_sq * second_z + double_sin * mixed
    across_axis = second_x + second_z - along_axis
    return along_axis, across_axis


def leapfrog(extended, former, coefficients):
    courant_sq, epsilon, delta_value, sine_sq, cosine_sq, double_sin = coefficients
    along_p, across_p = derivatives(extended[0], sine_sq, cosine_sq, double_sin)
    along_q, across_q = derivatives(extended[1], sine_sq, cosine_sq, double_sin)
    pressure = extended[0][..., 1:-1, :]
    auxiliary = extended[1][..., 1:-1, :]
    pressure_next = 2.0 * pressure - former[0] + courant_sq * ((1.0 + 2.0 * epsilon) * across_p + along_q)
    auxiliary_next = 2.0 * auxiliary - former[1] + courant_sq * ((1.0 + 2.0 * delta_value) * across_p + along_q)
    return jnp.stack([pressure_next, auxiliary_next])


def reference(pressure, auxiliary, pressure_prior, auxiliary_prior, courant_sq, thomsen_epsilon, thomsen_delta, tilt_angle, frequencies, spectra, target_cells, patch_lists, patch_counts):
    sine_sq, cosine_sq, double_sin = tilt_terms(tilt_angle)
    coefficients = (courant_sq, thomsen_epsilon, thomsen_delta, sine_sq, cosine_sq, double_sin)
    brick_of = jnp.arange(TARGETS, dtype=jnp.int32) // TGT_BRICK
    global_cells = (brick_of * (CX * CZ) + target_cells).astype(jnp.int32)

    def propagate(fields):
        current = jnp.stack([fields[0], fields[1]])
        former = jnp.stack([fields[2], fields[3]])
        samples = []
        for moment in range(STEPS):
            extended = jnp.pad(current, ((0, 0), (1, 1), (0, 0)))
            advanced = leapfrog(extended, former, coefficients)
            former = current
            current = advanced
            samples.append(current[0].reshape(-1)[global_cells])
        return current[0], current[1], jnp.stack(samples)

    pressure_out, auxiliary_out, samples = lax.map(propagate, (pressure, auxiliary, pressure_prior, auxiliary_prior))
    spectra_out = spectra
    for moment in range(STEPS):
        angle = frequencies * (moment + 1.0)
        table = jnp.concatenate([jnp.cos(angle), -jnp.sin(angle)])
        spectra_out = spectra_out + table[None, :, None] * samples[:, moment][:, None, :]
    features = spectra_out.astype(jnp.bfloat16).reshape(SHOTS * 2 * FREQ, TARGETS)

    def brick_tiles(brick_index):
        lists = lax.dynamic_index_in_dim(patch_lists, brick_index, 0, keepdims=False)
        columns = (lists + brick_index * TGT_BRICK).astype(jnp.int32).reshape(-1)
        chosen = jnp.take(features, columns, axis=1).astype(jnp.float32).reshape(FEATURES, GROUPS, P_MAX, PATCH)
        grams = jnp.einsum('fgpa,fgpb->gpab', chosen, chosen) / FEATURES
        counts = lax.dynamic_index_in_dim(patch_counts, brick_index, 0, keepdims=False)
        live_slots = (jnp.arange(P_MAX, dtype=jnp.int32)[None, :] < counts[:, None]).astype(jnp.float32)
        return grams * live_slots[:, :, None, None]

    gram_tiles = lax.map(brick_tiles, jnp.arange(BRICKS, dtype=jnp.int32))
    return pressure_out, auxiliary_out, spectra_out, gram_tiles
```

```python
import functools

import jax
import jax.numpy as jnp
from jax import lax
from jax.experimental import pallas as pl
from jax.experimental.pallas import tpu as pltpu
from jax.sharding import PartitionSpec as P

STEPS = 4
PATCH = 128
P_MAX = 3
SHOTS = 8
ROWS = 32
HALO = 4
DEPTH = 512
TILES = DEPTH // 128
CHIPS = 8
CHUNK = 80
MESH = pl.DeviceIdType.MESH
F32 = jnp.float32
BF16 = jnp.bfloat16

FAR_FIRST = (4, 3, 5, 2, 6, 1, 7)
NEAR_FIRST = (1, 7, 2, 6, 3, 5, 4)


def split(value):
    high = value.astype(BF16)
    return high, (value - high.astype(F32)).astype(BF16)


def kernel(
    bricks,
    freq_ref,
    counts_ref,
    courant_ref,
    epsilon_ref,
    delta_ref,
    tilt_ref,
    cells_ref,
    lists_ref,
    p_in,
    q_in,
    pp_in,
    qq_in,
    spectra_in,
    p_out,
    q_out,
    spectra_out,
    gram_ref,
    pbuf,
    qbuf,
    coef,
    slab_out,
    slab_in,
    rim_out,
    rim_in,
    spec,
    onehot,
    samples,
    feats,
    half,
    part_in,
    gathered,
    in_sem,
    out_sem,
    halo_send,
    halo_recv,
    feat_send,
    feat_recv,
    part_send,
    part_recv,
    ring_send,
    ring_recv,
    pass_send,
    pass_recv,
):
    shot = lax.axis_index("shot")
    brick = lax.axis_index("brick")
    chip = shot // 2
    core = lax.rem(shot, 2)
    has_left = brick > 0
    has_right = brick < bricks - 1

    barrier = pltpu.get_barrier_semaphore()
    for other in range(1, 2 * CHIPS):
        pl.semaphore_signal(
            barrier,
            inc=1,
            device_id={"shot": lax.rem(shot + other, 2 * CHIPS)},
            device_id_type=MESH,
        )

    @pl.when(has_left)
    def _():
        pl.semaphore_signal(barrier, inc=1, device_id={"brick": brick - 1}, device_id_type=MESH)

    @pl.when(has_right)
    def _():
        pl.semaphore_signal(barrier, inc=1, device_id={"brick": brick + 1}, device_id_type=MESH)

    loads = []
    for number, (source, target, slot) in enumerate(
        ((p_in, pbuf, 1), (q_in, qbuf, 1), (pp_in, pbuf, 0), (qq_in, qbuf, 0))
    ):
        for s in range(SHOTS):
            loads.append(
                pltpu.make_async_copy(
                    source.at[s],
                    target.at[slot, pl.ds(HALO, ROWS), s],
                    in_sem.at[number],
                )
            )
    for load in loads:
        load.start()
    spectra_load = pltpu.make_async_copy(spectra_in, spec, in_sem.at[4])
    spectra_load.start()

    sine = jnp.sin(tilt_ref[...])
    cosine = jnp.cos(tilt_ref[...])
    courant = courant_ref[...]
    own = pl.ds(8, ROWS)
    coef[0, own] = cosine * cosine
    coef[1, own] = 0.5 * sine * cosine
    coef[2, own] = courant
    coef[3, own] = courant * (1.0 + 2.0 * epsilon_ref[...])
    coef[4, own] = courant * (1.0 + 2.0 * delta_ref[...])
    for number in range(5):
        rim_out[0, pl.ds(3 * number, 3)] = coef[number, pl.ds(8, 3)]
        rim_out[1, pl.ds(3 * number, 3)] = coef[number, pl.ds(8 + ROWS - 3, 3)]
    rim_out[0, pl.ds(15, 1)] = jnp.zeros((1, DEPTH), F32)
    rim_out[1, pl.ds(15, 1)] = jnp.zeros((1, DEPTH), F32)

    for load in loads:
        load.wait()
    for side in range(2):
        first = HALO if side == 0 else HALO + ROWS - 4
        for row in range(4):
            slab_out[side, row] = jnp.concatenate(
                [pbuf[1, first + row], qbuf[1, first + row]], axis=0
            ).astype(BF16)
        first = HALO if side == 0 else HALO + ROWS - 3
        for row in range(3):
            slab_out[side, 4 + row] = jnp.concatenate(
                [pbuf[0, first + row], qbuf[0, first + row]], axis=0
            ).astype(BF16)

    pl.semaphore_wait(
        barrier, 2 * CHIPS - 1 + has_left.astype(jnp.int32) + has_right.astype(jnp.int32)
    )

    def halo_copies(side):
        target = {"brick": brick - 1 if side == 0 else brick + 1}
        return [
            pltpu.make_async_remote_copy(
                src_ref=slab_out.at[side],
                dst_ref=slab_in.at[1 - side],
                send_sem=halo_send.at[side, 0],
                recv_sem=halo_recv.at[1 - side, 0],
                device_id=target,
                device_id_type=MESH,
            ),
            pltpu.make_async_remote_copy(
                src_ref=rim_out.at[side],
                dst_ref=rim_in.at[1 - side],
                send_sem=halo_send.at[side, 1],
                recv_sem=halo_recv.at[1 - side, 1],
                device_id=target,
                device_id_type=MESH,
            ),
        ]

    for side, there in ((0, has_left), (1, has_right)):

        @pl.when(there)
        def _():
            for copy in halo_copies(side):
                copy.start()

    lane = lax.broadcasted_iota(jnp.int32, (SHOTS, 128), 1)
    first_lane = lane == 0
    last_lane = lane == 127

    def tiles(value):
        return [value[:, 128 * k : 128 * (k + 1)] for k in range(TILES)]

    def deeper(value):
        turned = [pltpu.roll(tile, 127, 1) for tile in value]
        turned.append(jnp.zeros((SHOTS, 128), F32))
        return [jnp.where(last_lane, turned[k + 1], turned[k]) for k in range(TILES)]

    def shallower(value):
        turned = [jnp.zeros((SHOTS, 128), F32)] + [pltpu.roll(tile, 1, 1) for tile in value]
        return [jnp.where(first_lane, turned[k], turned[k + 1]) for k in range(TILES)]

    def stencil(above, here, below):
        steep = [b + a for a, b in zip(above, below)]
        slope = [b - a for a, b in zip(above, below)]
        deep = [a + b for a, b in zip(deeper(here), shallower(here))]
        cross = [a - b for a, b in zip(deeper(slope), shallower(slope))]
        return steep, deep, cross

    def two_rows(moment, row):
        p_rows = [tiles(pbuf[moment, row + k]) for k in range(-1, 3)]
        q_rows = [tiles(qbuf[moment, row + k]) for k in range(-1, 3)]
        for k in range(2):
            at = row + k
            cos_sq, twist, speed, speed_e, speed_d = (
                tiles(jnp.broadcast_to(coef[number, pl.ds(at + 4, 1)], (SHOTS, DEPTH)))
                for number in range(5)
            )
            p_steep, p_deep, p_cross = stencil(p_rows[k], p_rows[k + 1], p_rows[k + 2])
            q_steep, q_deep, q_cross = stencil(q_rows[k], q_rows[k + 1], q_rows[k + 2])
            p_old = tiles(pbuf[moment - 1, at])
            q_old = tiles(qbuf[moment - 1, at])
            for t in range(TILES):
                p_two = p_rows[k + 1][t] + p_rows[k + 1][t]
                q_two = q_rows[k + 1][t] + q_rows[k + 1][t]
                sin_sq = 1.0 - cos_sq[t]
                across = cos_sq[t] * p_steep[t] + sin_sq * p_deep[t] - twist[t] * p_cross[t] - p_two
                along = sin_sq * q_steep[t] + cos_sq[t] * q_deep[t] + twist[t] * q_cross[t] - q_two
                push = speed[t] * along
                lanes = pl.ds(128 * t, 128)
                pbuf[moment + 1, at, :, lanes] = (p_two - p_old[t]) + (speed_e[t] * across + push)
                qbuf[moment + 1, at, :, lanes] = (q_two - q_old[t]) + (speed_d[t] * across + push)

    def inner_step(moment, carry):
        def pair(number, carry):
            two_rows(moment, moment + HALO + 2 * number)
            return carry

        return lax.fori_loop(0, ROWS // 2 - moment, pair, carry)

    lax.fori_loop(1, STEPS + 1, inner_step, 0)

    cells = cells_ref[...]
    target_x = cells >> 9
    target_z = cells & (DEPTH - 1)
    onehot[...] = (
        lax.broadcasted_iota(jnp.int32, (DEPTH, DEPTH), 0) == target_z
    ).astype(F32).astype(BF16)

    def picked(moment, first, count):
        rows = pbuf[moment + 1, pl.ds(first + HALO, count)].reshape(count * SHOTS, DEPTH)
        high, low = split(rows)
        values = jnp.dot(high, onehot[...], preferred_element_type=F32) + jnp.dot(
            low, onehot[...], preferred_element_type=F32
        )
        total = jnp.zeros((SHOTS, DEPTH), F32)
        for k in range(count):
            total = total + jnp.where(
                target_x == first + k, values[k * SHOTS : (k + 1) * SHOTS], 0.0
            )
        return total

    def inner_samples(moment, carry):
        samples[moment - 1] = picked(moment, HALO, ROWS - 2 * HALO)
        return carry

    lax.fori_loop(1, STEPS + 1, inner_samples, 0)

    number = lax.broadcasted_iota(jnp.int32, (16, 128), 0)
    frequency = jnp.zeros((16, 128), F32)
    for k in range(16):
        frequency = jnp.where(number == k, freq_ref[k], frequency)
    tables = []
    for moment in range(STEPS):
        angle = frequency * (moment + 1.0)
        tables.append(jnp.concatenate([jnp.cos(angle), -jnp.sin(angle)], axis=0))

    for side, there in ((0, has_left), (1, has_right)):

        @pl.when(there)
        def _():
            for copy in halo_copies(1 - side):
                copy.wait_recv()

        @pl.when(jnp.logical_not(there))
        def _():
            slab_in[side] = jnp.zeros((7, 16, DEPTH), BF16)
            rim_in[side] = jnp.zeros((16, DEPTH), F32)

    for side in range(2):
        first = 0 if side == 0 else HALO + ROWS
        for row in range(4):
            both = slab_in[side, row].astype(F32)
            pbuf[1, first + row] = both[:SHOTS]
            qbuf[1, first + row] = both[SHOTS:]
        first = 1 if side == 0 else HALO + ROWS
        for row in range(3):
            both = slab_in[side, 4 + row].astype(F32)
            pbuf[0, first + row] = both[:SHOTS]
            qbuf[0, first + row] = both[SHOTS:]
        for k in range(5):
            coef[k, pl.ds(first + 4, 3)] = rim_in[side, pl.ds(3 * k, 3)]

    def outer_step(moment, carry):
        def pair(number, carry):
            two_rows(
                moment,
                jnp.where(number < 2, moment + 2 * number, ROWS - moment + 2 * number),
            )
            return carry

        return lax.fori_loop(0, 4, pair, carry)

    lax.fori_loop(1, STEPS + 1, outer_step, 0)

    stores = []
    for number, (source, target) in enumerate(((pbuf, p_out), (qbuf, q_out))):
        for s in range(SHOTS):
            stores.append(
                pltpu.make_async_copy(
                    source.at[STEPS + 1, pl.ds(HALO, ROWS), s],
                    target.at[s],
                    out_sem.at[number],
                )
            )
    for store in stores:
        store.start()

    def outer_samples(moment, carry):
        samples[moment - 1] = (
            samples[moment - 1] + picked(moment, 0, HALO) + picked(moment, ROWS - HALO, HALO)
        )
        return carry

    lax.fori_loop(1, STEPS + 1, outer_samples, 0)

    spectra_load.wait()

    def transform(s, carry):
        drawn = [samples[moment, pl.ds(s, 1)] for moment in range(STEPS)]
        for t in range(TILES):
            lanes = pl.ds(128 * t, 128)
            value = spec[s, :, lanes]
            for moment in range(STEPS):
                value = value + tables[moment] * drawn[moment][:, 128 * t : 128 * (t + 1)]
            spec[s, :, lanes] = value
            feats[core, pl.ds(s * 32, 32), lanes] = value.astype(BF16)
        return carry

    lax.fori_loop(0, SHOTS, transform, 0)
    spectra_store = pltpu.make_async_copy(spec, spectra_out, out_sem.at[2])
    spectra_store.start()

    mate = {"shot": 2 * chip + 1 - core}
    feat_copy = pltpu.make_async_remote_copy(
        src_ref=feats.at[core],
        dst_ref=feats.at[core],
        send_sem=feat_send,
        recv_sem=feat_recv,
        device_id=mate,
        device_id_type=MESH,
    )
    feat_copy.start()
    feat_copy.wait_recv()

    blocks = [
        feats[:, :, pl.ds(pl.multiple_of(lax.rem(core + k, 4) * 128, 128), 128)].reshape(512, 128)
        for k in range(4)
    ]
    products = []
    for left, right in (((0), (0, 1, 2)), ((2), (2, 3))):
        product = lax.dot_general(
            blocks[left],
            jnp.concatenate([blocks[k] for k in right], axis=1),
            (((0,), (0,)), ((), ())),
            preferred_element_type=F32,
        )
        products += [product[:, 128 * k : 128 * (k + 1)] for k in range(len(right))]

    for k in range(5):
        half[pl.ds(128 * k, 128)] = products[k]

    def rows_of(place):
        return pl.ds(pl.multiple_of(place * CHUNK, 8), CHUNK)

    def part_copy(place):
        return pltpu.make_async_remote_copy(
            src_ref=half.at[rows_of(place)],
            dst_ref=part_in.at[chip],
            send_sem=part_send.at[place],
            recv_sem=part_recv.at[chip],
            device_id={"shot": 2 * place + core},
            device_id_type=MESH,
        )

    def part_arrival(place):
        return pltpu.make_async_remote_copy(
            src_ref=half.at[rows_of(place)],
            dst_ref=part_in.at[place],
            send_sem=part_send.at[place],
            recv_sem=part_recv.at[place],
            device_id={"shot": 2 * place + core},
            device_id_type=MESH,
        )

    for hop in FAR_FIRST:
        part_copy(lax.rem(chip + hop, CHIPS)).start()
    total = half[rows_of(chip)]
    for hop in NEAR_FIRST:
        place = lax.rem(chip + hop, CHIPS)
        part_arrival(place).wait_recv()
        total = total + part_in[place]
    gathered[core, rows_of(chip)] = total

    def ring_copy(owner, place):
        return pltpu.make_async_remote_copy(
            src_ref=gathered.at[core, rows_of(owner)],
            dst_ref=gathered.at[core, rows_of(owner)],
            send_sem=ring_send.at[place],
            recv_sem=ring_recv.at[owner],
            device_id={"shot": 2 * place + core},
            device_id_type=MESH,
        )

    def pass_copy(owner, which):
        return pltpu.make_async_remote_copy(
            src_ref=gathered.at[which, rows_of(owner)],
            dst_ref=gathered.at[which, rows_of(owner)],
            send_sem=pass_send.at[owner],
            recv_sem=pass_recv.at[owner],
            device_id=mate,
            device_id_type=MESH,
        )

    for hop in FAR_FIRST:
        ring_copy(chip, lax.rem(chip + hop, CHIPS)).start()
    pass_copy(chip, core).start()

    own_lists = lists_ref[shot]
    chosen = jnp.concatenate(
        [
            (lax.broadcasted_iota(jnp.int32, (512, PATCH), 0) == own_lists[p : p + 1])
            .astype(F32)
            .astype(BF16)
            for p in range(P_MAX)
        ],
        axis=1,
    )

    for hop in NEAR_FIRST:
        place = lax.rem(chip + hop, CHIPS)
        ring_copy(place, place).wait_recv()
        pass_copy(place, core).start()
    for hop in (0,) + NEAR_FIRST:
        pass_copy(lax.rem(chip + hop, CHIPS), 1 - core).wait_recv()

    strips = [None] * 4
    for which in range(2):
        grid = [gathered[which, pl.ds(128 * k, 128)] for k in range(5)]
        rows = [chosen[128 * (k % 4) : 128 * (k % 4 + 1)] for k in range(which, which + 4)]
        for row, left, right in (
            (which, [0.5 * grid[0], grid[1], grid[2]], rows[0:3]),
            (which + 2, [0.5 * grid[3], grid[4]], rows[2:4]),
        ):
            high, low = split(jnp.concatenate(left, axis=1))
            right = jnp.concatenate(right, axis=0)
            strips[row] = jnp.dot(high, right, preferred_element_type=F32) + jnp.dot(
                low, right, preferred_element_type=F32
            )
    strip_high, strip_low = split(jnp.concatenate(strips, axis=0))
    for p in range(P_MAX):
        lanes = slice(PATCH * p, PATCH * (p + 1))
        dims = (((0,), (0,)), ((), ()))
        tile = lax.dot_general(
            chosen[:, lanes], strip_high[:, lanes], dims, preferred_element_type=F32
        ) + lax.dot_general(
            chosen[:, lanes], strip_low[:, lanes], dims, preferred_element_type=F32
        )
        live = (counts_ref[0, 0] > p).astype(F32) * (1.0 / (2 * CHIPS * SHOTS * 32))
        gram_ref[p] = (tile + tile.T) * live

    for side, there in ((0, has_left), (1, has_right)):

        @pl.when(there)
        def _():
            for copy in halo_copies(side):
                copy.wait_send()

    feat_copy.wait_send()
    for hop in FAR_FIRST:
        place = lax.rem(chip + hop, CHIPS)
        part_copy(place).wait_send()
        ring_copy(chip, place).wait_send()
    for hop in (0,) + NEAR_FIRST:
        pass_copy(lax.rem(chip + hop, CHIPS), core).wait_send()
    for store in stores:
        store.wait()
    spectra_store.wait()


def shards(
    bricks,
    pressure,
    auxiliary,
    pressure_prior,
    auxiliary_prior,
    courant_sq,
    thomsen_epsilon,
    thomsen_delta,
    tilt_angle,
    frequencies,
    spectra,
    target_cells,
    patch_lists,
    patch_counts,
):
    vmem = pl.BlockSpec(memory_space=pltpu.VMEM)
    smem = pl.BlockSpec(memory_space=pltpu.SMEM)
    whole = pl.BlockSpec(memory_space=pl.ANY)
    field = jax.ShapeDtypeStruct((SHOTS, ROWS, DEPTH), F32)
    dma = pltpu.SemaphoreType.DMA
    p_out, q_out, spectra_out, gram = pl.pallas_call(
        functools.partial(kernel, bricks),
        out_shape=(field, field, field, jax.ShapeDtypeStruct((P_MAX, PATCH, PATCH), F32)),
        in_specs=[smem, smem] + [vmem] * 6 + [whole] * 5,
        out_specs=(whole, whole, whole, vmem),
        scratch_shapes=[
            pltpu.VMEM((STEPS + 2, ROWS + 2 * HALO, SHOTS, DEPTH), F32),
            pltpu.VMEM((STEPS + 2, ROWS + 2 * HALO, SHOTS, DEPTH), F32),
            pltpu.VMEM((5, ROWS + 16, DEPTH), F32),
            pltpu.VMEM((2, 7, 16, DEPTH), BF16),
            pltpu.VMEM((2, 7, 16, DEPTH), BF16),
            pltpu.VMEM((2, 16, DEPTH), F32),
            pltpu.VMEM((2, 16, DEPTH), F32),
            pltpu.VMEM((SHOTS, 32, DEPTH), F32),
            pltpu.VMEM((DEPTH, DEPTH), BF16),
            pltpu.VMEM((STEPS, SHOTS, DEPTH), F32),
            pltpu.VMEM((2, SHOTS * 32, DEPTH), BF16),
            pltpu.VMEM((CHIPS * CHUNK, 128), F32),
            pltpu.VMEM((CHIPS, CHUNK, 128), F32),
            pltpu.VMEM((2, CHIPS * CHUNK, 128), F32),
            dma((5,)),
            dma((3,)),
            dma((2, 2)),
            dma((2, 2)),
            dma,
            dma,
            dma((CHIPS,)),
            dma((CHIPS,)),
            dma((CHIPS,)),
            dma((CHIPS,)),
            dma((CHIPS,)),
            dma((CHIPS,)),
        ],
        compiler_params=pltpu.CompilerParams(collective_id=0, has_side_effects=True),
    )(
        frequencies,
        patch_counts,
        courant_sq,
        thomsen_epsilon,
        thomsen_delta,
        tilt_angle,
        target_cells.reshape(1, -1),
        patch_lists[0],
        pressure,
        auxiliary,
        pressure_prior,
        auxiliary_prior,
        spectra,
    )
    return p_out, q_out, spectra_out, gram.reshape(1, 1, P_MAX, PATCH, PATCH)


def solution(mesh):
    return jax.shard_map(
        functools.partial(shards, mesh.shape["brick"]),
        mesh=mesh,
        in_specs=(
            P("shot", "brick", None),
            P("shot", "brick", None),
            P("shot", "brick", None),
            P("shot", "brick", None),
            P("brick", None),
            P("brick", None),
            P("brick", None),
            P("brick", None),
            P(),
            P("shot", None, "brick"),
            P("brick"),
            P("brick", None, None, None),
            P("brick", "shot"),
        ),
        out_specs=(
            P("shot", "brick", None),
            P("shot", "brick", None),
            P("shot", None, "brick"),
            P("brick", "shot", None, None, None),
        ),
        check_vma=False,
    )
```

```python
import functools

import jax
import jax.numpy as jnp
from jax import lax
from jax.experimental import pallas as pl
from jax.experimental.pallas import tpu as pltpu
from jax.sharding import PartitionSpec as P

STEPS = 4
PATCH = 128
P_MAX = 3
SHOTS = 8
ROWS = 32
HALO = 4
DEPTH = 512
TILES = DEPTH // 128
CHIPS = 8
CHUNK = 128 // CHIPS
FULL = 178.0
MESH = pl.DeviceIdType.MESH
F32 = jnp.float32
BF16 = jnp.bfloat16

FAR_FIRST = (4, 3, 5, 2, 6, 1, 7)
NEAR_FIRST = (1, 7, 2, 6, 3, 5, 4)


def split(value):
    high = value.astype(BF16)
    return high, (value - high.astype(F32)).astype(BF16)


def kernel(
    bricks,
    freq_ref,
    counts_ref,
    courant_ref,
    epsilon_ref,
    delta_ref,
    tilt_ref,
    cells_ref,
    lists_ref,
    p_in,
    q_in,
    pp_in,
    qq_in,
    spectra_in,
    pbuf,
    qbuf,
    spec,
    gram_ref,
    coef,
    slab_out,
    slab_in,
    rim_out,
    rim_in,
    onehot,
    samples,
    feats,
    energy,
    half,
    part_out,
    part_in,
    gathered,
    in_sem,
    halo_send,
    halo_recv,
    feat_send,
    feat_recv,
    energy_send,
    energy_recv,
    part_send,
    part_recv,
    ring_send,
    ring_recv,
    pass_send,
    pass_recv,
):
    shot = lax.axis_index("shot")
    brick = lax.axis_index("brick")
    chip = shot // 2
    core = lax.rem(shot, 2)
    has_left = brick > 0
    has_right = brick < bricks - 1

    barrier = pltpu.get_barrier_semaphore()
    for other in range(1, 2 * CHIPS):
        pl.semaphore_signal(
            barrier,
            inc=1,
            device_id={"shot": lax.rem(shot + other, 2 * CHIPS)},
            device_id_type=MESH,
        )

    @pl.when(has_left)
    def _():
        pl.semaphore_signal(barrier, inc=1, device_id={"brick": brick - 1}, device_id_type=MESH)

    @pl.when(has_right)
    def _():
        pl.semaphore_signal(barrier, inc=1, device_id={"brick": brick + 1}, device_id_type=MESH)

    loads = []
    for number, (source, target, slot) in enumerate(
        ((p_in, pbuf, 1), (q_in, qbuf, 1), (pp_in, pbuf, 0), (qq_in, qbuf, 0))
    ):
        for s in range(SHOTS):
            loads.append(
                pltpu.make_async_copy(
                    source.at[s],
                    target.at[slot, pl.ds(HALO, ROWS), s],
                    in_sem.at[number],
                )
            )
    for load in loads:
        load.start()
    spectra_load = pltpu.make_async_copy(spectra_in, spec, in_sem.at[4])
    spectra_load.start()

    sine = jnp.sin(tilt_ref[...])
    cosine = jnp.cos(tilt_ref[...])
    courant = courant_ref[...]
    own = pl.ds(8, ROWS)
    coef[0, own] = cosine * cosine
    coef[1, own] = sine * sine
    coef[2, own] = 0.5 * sine * cosine
    coef[3, own] = courant
    coef[4, own] = courant * (1.0 + 2.0 * epsilon_ref[...])
    coef[5, own] = courant * (1.0 + 2.0 * delta_ref[...])
    for number in range(6):
        rim_out[0, pl.ds(4 * number, 3)] = coef[number, pl.ds(8, 3)]
        rim_out[1, pl.ds(4 * number, 3)] = coef[number, pl.ds(8 + ROWS - 3, 3)]
        rim_out[:, pl.ds(4 * number + 3, 1)] = jnp.zeros((2, 1, DEPTH), F32)

    for load in loads:
        load.wait()
    for side in range(2):
        first = HALO if side == 0 else HALO + ROWS - 4
        for row in range(4):
            slab_out[side, row] = jnp.concatenate(
                [pbuf[1, first + row], qbuf[1, first + row]], axis=0
            ).astype(BF16)
        first = HALO if side == 0 else HALO + ROWS - 3
        for row in range(3):
            slab_out[side, 4 + row] = jnp.concatenate(
                [pbuf[0, first + row], qbuf[0, first + row]], axis=0
            ).astype(BF16)

    pl.semaphore_wait(
        barrier, 2 * CHIPS - 1 + has_left.astype(jnp.int32) + has_right.astype(jnp.int32)
    )

    def halo_copies(side):
        target = {"brick": brick - 1 if side == 0 else brick + 1}
        return [
            pltpu.make_async_remote_copy(
                src_ref=slab_out.at[side],
                dst_ref=slab_in.at[1 - side],
                send_sem=halo_send.at[side, 0],
                recv_sem=halo_recv.at[1 - side, 0],
                device_id=target,
                device_id_type=MESH,
            ),
            pltpu.make_async_remote_copy(
                src_ref=rim_out.at[side],
                dst_ref=rim_in.at[1 - side],
                send_sem=halo_send.at[side, 1],
                recv_sem=halo_recv.at[1 - side, 1],
                device_id=target,
                device_id_type=MESH,
            ),
        ]

    for side, there in ((0, has_left), (1, has_right)):

        @pl.when(there)
        def _():
            for copy in halo_copies(side):
                copy.start()

    lane = lax.broadcasted_iota(jnp.int32, (SHOTS, 128), 1)
    first_lane = lane == 0
    last_lane = lane == 127

    def tiles(value):
        return [value[:, 128 * k : 128 * (k + 1)] for k in range(TILES)]

    def deeper(value):
        turned = [pltpu.roll(tile, 127, 1) for tile in value]
        turned.append(jnp.zeros((SHOTS, 128), F32))
        return [jnp.where(last_lane, turned[k + 1], turned[k]) for k in range(TILES)]

    def shallower(value):
        turned = [jnp.zeros((SHOTS, 128), F32)] + [pltpu.roll(tile, 1, 1) for tile in value]
        return [jnp.where(first_lane, turned[k], turned[k + 1]) for k in range(TILES)]

    def stencil(above, here, below):
        steep = [b + a for a, b in zip(above, below)]
        slope = [b - a for a, b in zip(above, below)]
        deep = [a + b for a, b in zip(deeper(here), shallower(here))]
        cross = [a - b for a, b in zip(deeper(slope), shallower(slope))]
        return steep, deep, cross

    def some_rows(moment, row, count):
        p_rows = [tiles(pbuf[moment, row + k]) for k in range(-1, count + 1)]
        q_rows = [tiles(qbuf[moment, row + k]) for k in range(-1, count + 1)]
        for k in range(count):
            at = row + k
            cos_sq, sin_sq, twist, speed, speed_e, speed_d = (
                tiles(jnp.broadcast_to(coef[number, pl.ds(at + 4, 1)], (SHOTS, DEPTH)))
                for number in range(6)
            )
            p_steep, p_deep, p_cross = stencil(p_rows[k], p_rows[k + 1], p_rows[k + 2])
            q_steep, q_deep, q_cross = stencil(q_rows[k], q_rows[k + 1], q_rows[k + 2])
            p_old = tiles(pbuf[moment - 1, at])
            q_old = tiles(qbuf[moment - 1, at])
            for t in range(TILES):
                p_two = p_rows[k + 1][t] + p_rows[k + 1][t]
                q_two = q_rows[k + 1][t] + q_rows[k + 1][t]
                across = (
                    cos_sq[t] * p_steep[t] + sin_sq[t] * p_deep[t] - twist[t] * p_cross[t] - p_two
                )
                along = (
                    sin_sq[t] * q_steep[t] + cos_sq[t] * q_deep[t] + twist[t] * q_cross[t] - q_two
                )
                push = speed[t] * along
                lanes = pl.ds(128 * t, 128)
                pbuf[moment + 1, at, :, lanes] = (p_two - p_old[t]) + (speed_e[t] * across + push)
                qbuf[moment + 1, at, :, lanes] = (q_two - q_old[t]) + (speed_d[t] * across + push)

    def inner_step(moment, carry):
        def group(number, carry):
            some_rows(moment, moment + HALO + 4 * number, 4)
            return carry

        return lax.fori_loop(0, (ROWS - 2 * moment + 3) // 4, group, carry)

    lax.fori_loop(1, STEPS + 1, inner_step, 0)

    cells = cells_ref[...]
    target_x = cells >> 9
    target_z = cells & (DEPTH - 1)
    onehot[...] = (
        lax.broadcasted_iota(jnp.int32, (DEPTH, DEPTH), 0) == target_z
    ).astype(F32).astype(BF16)

    def picked(moment, first, count):
        rows = pbuf[moment + 1, pl.ds(first + HALO, count)].reshape(count * SHOTS, DEPTH)
        high, low = split(rows)
        values = jnp.dot(high, onehot[...], preferred_element_type=F32) + jnp.dot(
            low, onehot[...], preferred_element_type=F32
        )
        total = jnp.zeros((SHOTS, DEPTH), F32)
        for k in range(count):
            total = total + jnp.where(
                target_x == first + k, values[k * SHOTS : (k + 1) * SHOTS], 0.0
            )
        return total

    def inner_samples(moment, carry):
        samples[moment - 1] = picked(moment, HALO, ROWS - 2 * HALO)
        return carry

    lax.fori_loop(1, STEPS + 1, inner_samples, 0)

    number = lax.broadcasted_iota(jnp.int32, (16, 128), 0)
    frequency = jnp.zeros((16, 128), F32)
    for k in range(16):
        frequency = jnp.where(number == k, freq_ref[k], frequency)
    tables = []
    for moment in range(STEPS):
        angle = frequency * (moment + 1.0)
        tables.append(jnp.concatenate([jnp.cos(angle), -jnp.sin(angle)], axis=0))

    for side, there in ((0, has_left), (1, has_right)):

        @pl.when(there)
        def _():
            for copy in halo_copies(1 - side):
                copy.wait_recv()

        @pl.when(jnp.logical_not(there))
        def _():
            slab_in[side] = jnp.zeros((7, 16, DEPTH), BF16)
            rim_in[side] = jnp.zeros((24, DEPTH), F32)

    for side in range(2):
        first = 0 if side == 0 else HALO + ROWS
        for row in range(4):
            both = slab_in[side, row].astype(F32)
            pbuf[1, first + row] = both[:SHOTS]
            qbuf[1, first + row] = both[SHOTS:]
        first = 1 if side == 0 else HALO + ROWS
        for row in range(3):
            both = slab_in[side, 4 + row].astype(F32)
            pbuf[0, first + row] = both[:SHOTS]
            qbuf[0, first + row] = both[SHOTS:]
        for k in range(6):
            coef[k, pl.ds(first + 4, 3)] = rim_in[side, pl.ds(4 * k, 3)]

    def outer_step(moment, carry):
        def group(side, carry):
            some_rows(moment, jnp.where(side == 0, moment, HALO + ROWS - moment), 4)
            return carry

        return lax.fori_loop(0, 2, group, carry)

    lax.fori_loop(1, STEPS + 1, outer_step, 0)

    edges = jnp.concatenate(
        [
            pbuf[moment + 1, pl.ds(first + HALO, HALO)].reshape(HALO * SHOTS, DEPTH)
            for moment in range(1, STEPS + 1)
            for first in (0, ROWS - HALO)
        ],
        axis=0,
    )
    high, low = split(edges)
    values = jnp.dot(high, onehot[...], preferred_element_type=F32) + jnp.dot(
        low, onehot[...], preferred_element_type=F32
    )
    for moment in range(STEPS):
        total = samples[moment]
        for k in range(2 * HALO):
            x = k if k < HALO else ROWS - 2 * HALO + k
            start = (moment * 2 * HALO + k) * SHOTS
            total = total + jnp.where(target_x == x, values[start : start + SHOTS], 0.0)
        samples[moment] = total

    spectra_load.wait()

    def transform(s, carry):
        drawn = [samples[moment, pl.ds(s, 1)] for moment in range(STEPS)]
        for t in range(TILES):
            lanes = pl.ds(128 * t, 128)
            value = spec[s, :, lanes]
            for moment in range(STEPS):
                value = value + tables[moment] * drawn[moment][:, 128 * t : 128 * (t + 1)]
            spec[s, :, lanes] = value
            feats[core, pl.ds(s * 32, 32), lanes] = value.astype(BF16)
        return carry

    lax.fori_loop(0, SHOTS, transform, 0)

    mate = {"shot": 2 * chip + 1 - core}
    feat_copy = pltpu.make_async_remote_copy(
        src_ref=feats.at[core],
        dst_ref=feats.at[core],
        send_sem=feat_send,
        recv_sem=feat_recv,
        device_id=mate,
        device_id_type=MESH,
    )
    feat_copy.start()
    feat_copy.wait_recv()

    both = feats[...].reshape(2 * SHOTS * 32, DEPTH)
    energy[chip] = jnp.dot(
        jnp.ones((8, 2 * SHOTS * 32), BF16), both * both, preferred_element_type=F32
    )

    def energy_copy(place, owner):
        return pltpu.make_async_remote_copy(
            src_ref=energy.at[owner, pl.ds(0, 1)],
            dst_ref=energy.at[owner, pl.ds(0, 1)],
            send_sem=energy_send.at[place],
            recv_sem=energy_recv.at[owner],
            device_id={"shot": 2 * place + core},
            device_id_type=MESH,
        )

    for hop in FAR_FIRST:
        energy_copy(lax.rem(chip + hop, CHIPS), chip).start()

    def units(place):
        level = energy[place, pl.ds(0, 1)]
        inverse = jnp.where(level > 0.0, lax.rsqrt(level), 0.0)
        return level * inverse, inverse

    def in_order(row):
        straight = [row[:, 128 * k : 128 * (k + 1)] for k in range(4)]
        return [jnp.where(core == 0, straight[k], straight[(k + 1) % 4]) for k in range(4)]

    pairs = ((0, 0), (0, 1), (0, 2), (2, 2), (2, 3))
    blocks = [
        feats[:, :, pl.ds(pl.multiple_of(lax.rem(core + k, 4) * 128, 128), 128)].reshape(512, 128)
        for k in range(4)
    ]
    row_number = lax.broadcasted_iota(jnp.int32, (128, 128), 0)
    lane_number = lax.broadcasted_iota(jnp.int32, (128, 128), 1)

    def upright(row, first, count):
        here = lane_number[:count] == row_number[:count] + first
        return jnp.sum(jnp.where(here, row, 0.0), axis=1, keepdims=True)

    inverses = in_order(units(chip)[1])
    columns = {k: upright(inverses[k] * FULL, 0, 128) for k in (0, 2)}
    number = 0
    for left, right in ((0, (0, 1, 2)), (2, (2, 3))):
        product = lax.dot_general(
            blocks[left],
            jnp.concatenate([blocks[k] for k in right], axis=1),
            (((0,), (0,)), ((), ())),
            preferred_element_type=F32,
        )
        for k, block in enumerate(right):
            value = product[:, 128 * k : 128 * (k + 1)]
            half[number] = value
            part_out[number] = jnp.round(value * columns[left] * (inverses[block] * FULL)).astype(jnp.int16)
            number += 1

    def rows_of(place):
        return pl.ds(pl.multiple_of(place * CHUNK, CHUNK), CHUNK)

    def part_copy(place, owner):
        return pltpu.make_async_remote_copy(
            src_ref=part_out.at[:, rows_of(place)],
            dst_ref=part_in.at[owner],
            send_sem=part_send.at[place],
            recv_sem=part_recv.at[owner],
            device_id={"shot": 2 * place + core},
            device_id_type=MESH,
        )

    for hop in FAR_FIRST:
        part_copy(lax.rem(chip + hop, CHIPS), chip).start()

    start = chip * CHUNK
    total = [half[k, rows_of(chip)] for k in range(5)]
    for hop in NEAR_FIRST:
        place = lax.rem(chip + hop, CHIPS)
        energy_copy(place, place).wait_recv()
        roots = in_order(units(place)[0])
        columns = {k: upright(roots[k] * (1.0 / FULL), start, CHUNK) for k in (0, 2)}
        part_copy(place, place).wait_recv()
        for k, (left, right) in enumerate(pairs):
            total[k] = total[k] + part_in[place, k].astype(F32) * columns[left] * (roots[right] * (1.0 / FULL))

    level = energy[0, pl.ds(0, 1)]
    for k in range(1, CHIPS):
        level = level + energy[k, pl.ds(0, 1)]
    inverse = jnp.where(level > 0.0, lax.rsqrt(level), 0.0)
    root = level * inverse
    inverses = in_order(inverse)
    columns = {k: upright(inverses[k] * FULL, start, CHUNK) for k in (0, 2)}
    for k, (left, right) in enumerate(pairs):
        gathered[core, k, rows_of(chip)] = jnp.round(
            total[k] * columns[left] * (inverses[right] * FULL)
        ).astype(jnp.int16)

    def ring_copy(owner, place):
        return pltpu.make_async_remote_copy(
            src_ref=gathered.at[core, :, rows_of(owner)],
            dst_ref=gathered.at[core, :, rows_of(owner)],
            send_sem=ring_send.at[place],
            recv_sem=ring_recv.at[owner],
            device_id={"shot": 2 * place + core},
            device_id_type=MESH,
        )

    def pass_copy(owner, which):
        return pltpu.make_async_remote_copy(
            src_ref=gathered.at[which, :, rows_of(owner)],
            dst_ref=gathered.at[which, :, rows_of(owner)],
            send_sem=pass_send.at[owner],
            recv_sem=pass_recv.at[owner],
            device_id=mate,
            device_id_type=MESH,
        )

    for hop in FAR_FIRST:
        ring_copy(chip, lax.rem(chip + hop, CHIPS)).start()
    pass_copy(chip, core).start()

    chosen = jnp.concatenate(
        [
            (lax.broadcasted_iota(jnp.int32, (512, PATCH), 0) == lists_ref[p, pl.ds(shot, 1)])
            .astype(F32)
            .astype(BF16)
            for p in range(P_MAX)
        ],
        axis=1,
    )

    for hop in NEAR_FIRST:
        place = lax.rem(chip + hop, CHIPS)
        ring_copy(place, place).wait_recv()
        pass_copy(place, core).start()
    for hop in (0,) + NEAR_FIRST:
        pass_copy(lax.rem(chip + hop, CHIPS), 1 - core).wait_recv()

    strips = [None] * 4
    for which in range(2):
        grid = [gathered[which, k].astype(F32) for k in range(5)]
        rows = [chosen[128 * (k % 4) : 128 * (k % 4 + 1)] for k in range(which, which + 4)]
        for row, left, right in (
            (which, [0.5 * grid[0], grid[1], grid[2]], rows[0:3]),
            (which + 2, [0.5 * grid[3], grid[4]], rows[2:4]),
        ):
            high, low = split(jnp.concatenate(left, axis=1))
            right = jnp.concatenate(right, axis=0)
            strips[row] = jnp.dot(high, right, preferred_element_type=F32) + jnp.dot(
                low, right, preferred_element_type=F32
            )
    strip_high, strip_low = split(jnp.concatenate(strips, axis=0))
    root_high, root_low = split(jnp.broadcast_to(root * (1.0 / FULL), (8, DEPTH)))
    chosen_root = jnp.dot(root_high, chosen, preferred_element_type=F32) + jnp.dot(
        root_low, chosen, preferred_element_type=F32
    )
    for p in range(P_MAX):
        lanes = slice(PATCH * p, PATCH * (p + 1))
        dims = (((0,), (0,)), ((), ()))
        tile = lax.dot_general(
            chosen[:, lanes], strip_high[:, lanes], dims, preferred_element_type=F32
        ) + lax.dot_general(
            chosen[:, lanes], strip_low[:, lanes], dims, preferred_element_type=F32
        )
        live = (counts_ref[0, 0] > p).astype(F32) * (1.0 / (2 * CHIPS * SHOTS * 32))
        scale = chosen_root[0:1, lanes]
        gram_ref[p] = ((tile + tile.T) * scale).T * (scale * live)

    for side, there in ((0, has_left), (1, has_right)):

        @pl.when(there)
        def _():
            for copy in halo_copies(side):
                copy.wait_send()

    feat_copy.wait_send()
    for hop in FAR_FIRST:
        place = lax.rem(chip + hop, CHIPS)
        energy_copy(place, chip).wait_send()
        part_copy(place, chip).wait_send()
        ring_copy(chip, place).wait_send()
    for hop in (0,) + NEAR_FIRST:
        pass_copy(lax.rem(chip + hop, CHIPS), core).wait_send()


def deliver(pbuf, qbuf, spec, gram, p_out, q_out, spectra_out, gram_out, sem):
    copies = [
        pltpu.make_async_copy(spec, spectra_out, sem.at[2]),
        pltpu.make_async_copy(gram, gram_out, sem.at[3]),
    ]
    for number, (source, target) in enumerate(((pbuf, p_out), (qbuf, q_out))):
        for s in range(SHOTS):
            copies.append(
                pltpu.make_async_copy(
                    source.at[STEPS + 1, pl.ds(HALO, ROWS), s], target.at[s], sem.at[number]
                )
            )
    for copy in copies:
        copy.start()
    for copy in copies:
        copy.wait()


def shards(
    bricks,
    pressure,
    auxiliary,
    pressure_prior,
    auxiliary_prior,
    courant_sq,
    thomsen_epsilon,
    thomsen_delta,
    tilt_angle,
    frequencies,
    spectra,
    target_cells,
    patch_lists,
    patch_counts,
):
    vmem = pl.BlockSpec(memory_space=pltpu.VMEM)
    smem = pl.BlockSpec(memory_space=pltpu.SMEM)
    whole = pl.BlockSpec(memory_space=pltpu.HBM)
    history = pltpu.VMEM((STEPS + 2, ROWS + 2 * HALO, SHOTS, DEPTH), F32)
    dma = pltpu.SemaphoreType.DMA
    made = pl.pallas_call(
        functools.partial(kernel, bricks),
        out_shape=(
            history,
            history,
            pltpu.VMEM((SHOTS, 32, DEPTH), F32),
            pltpu.VMEM((P_MAX, PATCH, PATCH), F32),
        ),
        in_specs=[smem, smem] + [vmem] * 6 + [whole] * 5,
        out_specs=(vmem,) * 4,
        scratch_shapes=[
            pltpu.VMEM((6, ROWS + 16, DEPTH), F32),
            pltpu.VMEM((2, 7, 16, DEPTH), BF16),
            pltpu.VMEM((2, 7, 16, DEPTH), BF16),
            pltpu.VMEM((2, 24, DEPTH), F32),
            pltpu.VMEM((2, 24, DEPTH), F32),
            pltpu.VMEM((DEPTH, DEPTH), BF16),
            pltpu.VMEM((STEPS, SHOTS, DEPTH), F32),
            pltpu.VMEM((2, SHOTS * 32, DEPTH), BF16),
            pltpu.VMEM((CHIPS, 8, DEPTH), F32),
            pltpu.VMEM((5, 128, 128), F32),
            pltpu.VMEM((5, 128, 128), jnp.int16),
            pltpu.VMEM((CHIPS, 5, CHUNK, 128), jnp.int16),
            pltpu.VMEM((2, 5, 128, 128), jnp.int16),
            dma((5,)),
            dma((2, 2)),
            dma((2, 2)),
            dma,
            dma,
            dma((CHIPS,)),
            dma((CHIPS,)),
            dma((CHIPS,)),
            dma((CHIPS,)),
            dma((CHIPS,)),
            dma((CHIPS,)),
            dma((CHIPS,)),
            dma((CHIPS,)),
        ],
        compiler_params=pltpu.CompilerParams(
            collective_id=0, has_side_effects=True, vmem_limit_bytes=50 << 20
        ),
    )(
        frequencies,
        patch_counts,
        courant_sq,
        thomsen_epsilon,
        thomsen_delta,
        tilt_angle,
        target_cells.reshape(1, -1),
        jnp.transpose(patch_lists[0], (1, 0, 2)),
        pressure,
        auxiliary,
        pressure_prior,
        auxiliary_prior,
        spectra,
    )
    field = jax.ShapeDtypeStruct((SHOTS, ROWS, DEPTH), F32)
    p_out, q_out, spectra_out, gram = pl.pallas_call(
        deliver,
        out_shape=(field, field, field, jax.ShapeDtypeStruct((P_MAX, PATCH, PATCH), F32)),
        in_specs=[vmem] * 4,
        out_specs=(whole,) * 4,
        scratch_shapes=[dma((4,))],
        compiler_params=pltpu.CompilerParams(vmem_limit_bytes=8 << 20),
    )(*(pltpu.with_memory_space_constraint(array, pltpu.VMEM) for array in made))
    return p_out, q_out, spectra_out, gram.reshape(1, 1, P_MAX, PATCH, PATCH)


def solution(mesh):
    return jax.shard_map(
        functools.partial(shards, mesh.shape["brick"]),
        mesh=mesh,
        in_specs=(
            P("shot", "brick", None),
            P("shot", "brick", None),
            P("shot", "brick", None),
            P("shot", "brick", None),
            P("brick", None),
            P("brick", None),
            P("brick", None),
            P("brick", None),
            P(),
            P("shot", None, "brick"),
            P("brick"),
            P("brick", None, None, None),
            P("brick", "shot"),
        ),
        out_specs=(
            P("shot", "brick", None),
            P("shot", "brick", None),
            P("shot", None, "brick"),
            P("brick", "shot", None, None, None),
        ),
        check_vma=False,
    )
```

```python
import functools

import jax
import jax.numpy as jnp
from jax import lax
from jax.experimental import pallas as pl
from jax.experimental.pallas import tpu as pltpu
from jax.sharding import PartitionSpec as P

STEPS = 4
PATCH = 128
P_MAX = 3
SHOTS = 8
ROWS = 32
HALO = 4
DEPTH = 512
TILES = DEPTH // 128
CHIPS = 8
CHUNK = 128 // CHIPS
FULL = 178.0
MESH = pl.DeviceIdType.MESH
F32 = jnp.float32
BF16 = jnp.bfloat16

FAR_FIRST = (4, 3, 5, 2, 6, 1, 7)
NEAR_FIRST = (1, 7, 2, 6, 3, 5, 4)


def split(value):
    high = value.astype(BF16)
    return high, (value - high.astype(F32)).astype(BF16)


def kernel(
    bricks,
    freq_ref,
    counts_ref,
    courant_in,
    epsilon_in,
    delta_in,
    tilt_in,
    cells_ref,
    lists_ref,
    p_in,
    q_in,
    pp_in,
    qq_in,
    spectra_in,
    pbuf,
    qbuf,
    spec,
    gram_ref,
    model,
    coef,
    slab_out,
    slab_in,
    rim_out,
    rim_in,
    onehot,
    chosen,
    table,
    samples,
    feats,
    energy,
    half,
    part_out,
    part_in,
    gathered,
    in_sem,
    halo_send,
    halo_recv,
    feat_send,
    feat_recv,
    energy_send,
    energy_recv,
    part_send,
    part_recv,
    ring_send,
    ring_recv,
    pass_send,
    pass_recv,
):
    shot = lax.axis_index("shot")
    brick = lax.axis_index("brick")
    chip = shot // 2
    core = lax.rem(shot, 2)
    has_left = brick > 0
    has_right = brick < bricks - 1

    barrier = pltpu.get_barrier_semaphore()
    for other in range(1, 2 * CHIPS):
        pl.semaphore_signal(
            barrier,
            inc=1,
            device_id={"shot": lax.rem(shot + other, 2 * CHIPS)},
            device_id_type=MESH,
        )

    @pl.when(has_left)
    def _():
        pl.semaphore_signal(barrier, inc=1, device_id={"brick": brick - 1}, device_id_type=MESH)

    @pl.when(has_right)
    def _():
        pl.semaphore_signal(barrier, inc=1, device_id={"brick": brick + 1}, device_id_type=MESH)

    model_loads = [
        pltpu.make_async_copy(source, model.at[k], in_sem.at[5])
        for k, source in enumerate((courant_in, epsilon_in, delta_in, tilt_in))
    ]
    for load in model_loads:
        load.start()
    loads = []
    for number, (source, target, slot) in enumerate(
        ((p_in, pbuf, 1), (q_in, qbuf, 1), (pp_in, pbuf, 0), (qq_in, qbuf, 0))
    ):
        for s in range(SHOTS):
            loads.append(
                pltpu.make_async_copy(
                    source.at[s],
                    target.at[slot, pl.ds(HALO, ROWS), s],
                    in_sem.at[number],
                )
            )
    for load in loads:
        load.start()
    spectra_load = pltpu.make_async_copy(spectra_in, spec, in_sem.at[4])
    spectra_load.start()

    cells = cells_ref[...]
    target_x = cells >> 9
    target_z = cells & (DEPTH - 1)
    onehot[...] = (
        lax.broadcasted_iota(jnp.int32, (DEPTH, DEPTH), 0) == target_z
    ).astype(F32).astype(BF16)

    for p in range(P_MAX):
        chosen[:, pl.ds(PATCH * p, PATCH)] = (
            (lax.broadcasted_iota(jnp.int32, (512, PATCH), 0) == lists_ref[p, pl.ds(shot, 1)])
            .astype(F32)
            .astype(BF16)
        )

    number = lax.broadcasted_iota(jnp.int32, (16, 128), 0)
    frequency = jnp.zeros((16, 128), F32)
    for k in range(16):
        frequency = jnp.where(number == k, freq_ref[k], frequency)
    for moment in range(STEPS):
        angle = frequency * (moment + 1.0)
        table[moment, pl.ds(0, 16)] = jnp.cos(angle)
        table[moment, pl.ds(16, 16)] = -jnp.sin(angle)

    def shifted(value):
        lane = lax.broadcasted_iota(jnp.int32, value.shape, 1)
        return (
            jnp.where(lane == 0, 0.0, pltpu.roll(value, 1, 1)),
            jnp.where(lane == DEPTH - 1, 0.0, pltpu.roll(value, DEPTH - 1, 1)),
        )

    for load in model_loads:
        load.wait()
    sine = jnp.sin(model[3])
    cosine = jnp.cos(model[3])
    courant = model[0]
    own = pl.ds(8, ROWS)
    turns = (cosine * cosine, sine * sine, 0.5 * sine * cosine)
    for k, value in enumerate(turns):
        coef[k, own] = value
        coef[6 + k, own], coef[9 + k, own] = shifted(value)
    coef[3, own] = courant
    coef[4, own] = courant * (1.0 + 2.0 * model[1])
    coef[5, own] = courant * (1.0 + 2.0 * model[2])
    for number in range(6):
        rim_out[0, pl.ds(4 * number, 3)] = coef[number, pl.ds(8, 3)]
        rim_out[1, pl.ds(4 * number, 3)] = coef[number, pl.ds(8 + ROWS - 3, 3)]
        rim_out[:, pl.ds(4 * number + 3, 1)] = jnp.zeros((2, 1, DEPTH), F32)

    for load in loads:
        load.wait()
    for side in range(2):
        first = HALO if side == 0 else HALO + ROWS - 4
        for row in range(4):
            slab_out[side, row] = jnp.concatenate(
                [pbuf[1, first + row], qbuf[1, first + row]], axis=0
            ).astype(BF16)
        first = HALO if side == 0 else HALO + ROWS - 3
        for row in range(3):
            slab_out[side, 4 + row] = jnp.concatenate(
                [pbuf[0, first + row], qbuf[0, first + row]], axis=0
            ).astype(BF16)

    pl.semaphore_wait(
        barrier, 2 * CHIPS - 1 + has_left.astype(jnp.int32) + has_right.astype(jnp.int32)
    )

    def halo_copies(side):
        target = {"brick": brick - 1 if side == 0 else brick + 1}
        return [
            pltpu.make_async_remote_copy(
                src_ref=slab_out.at[side],
                dst_ref=slab_in.at[1 - side],
                send_sem=halo_send.at[side, 0],
                recv_sem=halo_recv.at[1 - side, 0],
                device_id=target,
                device_id_type=MESH,
            ),
            pltpu.make_async_remote_copy(
                src_ref=rim_out.at[side],
                dst_ref=rim_in.at[1 - side],
                send_sem=halo_send.at[side, 1],
                recv_sem=halo_recv.at[1 - side, 1],
                device_id=target,
                device_id_type=MESH,
            ),
        ]

    for side, there in ((0, has_left), (1, has_right)):

        @pl.when(there)
        def _():
            for copy in halo_copies(side):
                copy.start()

    lane = lax.broadcasted_iota(jnp.int32, (SHOTS, 128), 1)
    first_lane = lane == 0
    last_lane = lane == 127

    def tiles(value):
        return [value[:, 128 * k : 128 * (k + 1)] for k in range(TILES)]

    def deeper(value):
        turned = [pltpu.roll(tile, 127, 1) for tile in value]
        return [jnp.where(last_lane, turned[(k + 1) % TILES], turned[k]) for k in range(TILES)]

    def shallower(value):
        turned = [pltpu.roll(tile, 1, 1) for tile in value]
        return [jnp.where(first_lane, turned[k - 1], turned[k]) for k in range(TILES)]

    def mix(first, a, second, b, sign):
        if sign > 0:
            return [w * x + v * y for w, x, v, y in zip(first, a, second, b)]
        return [w * x - v * y for w, x, v, y in zip(first, a, second, b)]

    def some_rows(moment, row, count):
        p_rows = [tiles(pbuf[moment, row + k]) for k in range(-1, count + 1)]
        q_rows = [tiles(qbuf[moment, row + k]) for k in range(-1, count + 1)]
        for k in range(count):
            at = row + k
            (
                cos_sq,
                sin_sq,
                speed,
                speed_e,
                speed_d,
                cos_up,
                sin_up,
                twist_up,
                cos_down,
                sin_down,
                twist_down,
            ) = (
                tiles(jnp.broadcast_to(coef[number, pl.ds(at + 4, 1)], (SHOTS, DEPTH)))
                for number in (0, 1, 3, 4, 5, 6, 7, 8, 9, 10, 11)
            )
            p_steep = [a + b for a, b in zip(p_rows[k], p_rows[k + 2])]
            p_slope = [b - a for a, b in zip(p_rows[k], p_rows[k + 2])]
            q_steep = [a + b for a, b in zip(q_rows[k], q_rows[k + 2])]
            q_slope = [b - a for a, b in zip(q_rows[k], q_rows[k + 2])]
            p_deeper = deeper(mix(sin_up, p_rows[k + 1], twist_up, p_slope, -1))
            p_shallower = shallower(mix(sin_down, p_rows[k + 1], twist_down, p_slope, 1))
            q_deeper = deeper(mix(cos_up, q_rows[k + 1], twist_up, q_slope, 1))
            q_shallower = shallower(mix(cos_down, q_rows[k + 1], twist_down, q_slope, -1))
            p_old = tiles(pbuf[moment - 1, at])
            q_old = tiles(qbuf[moment - 1, at])
            for t in range(TILES):
                p_two = p_rows[k + 1][t] + p_rows[k + 1][t]
                q_two = q_rows[k + 1][t] + q_rows[k + 1][t]
                across = (cos_sq[t] * p_steep[t] - p_two) + (p_deeper[t] + p_shallower[t])
                along = (sin_sq[t] * q_steep[t] - q_two) + (q_deeper[t] + q_shallower[t])
                push = speed[t] * along
                lanes = pl.ds(128 * t, 128)
                pbuf[moment + 1, at, :, lanes] = (p_two - p_old[t]) + (speed_e[t] * across + push)
                qbuf[moment + 1, at, :, lanes] = (q_two - q_old[t]) + (speed_d[t] * across + push)

    def inner_step(moment, carry):
        def group(number, carry):
            some_rows(moment, moment + HALO + 4 * number, 4)
            return carry

        return lax.fori_loop(0, (ROWS - 2 * moment + 3) // 4, group, carry)

    lax.fori_loop(1, STEPS + 1, inner_step, 0)

    def picked(moment, first, count):
        rows = pbuf[moment + 1, pl.ds(first + HALO, count)].reshape(count * SHOTS, DEPTH)
        high, low = split(rows)
        values = jnp.dot(high, onehot[...], preferred_element_type=F32) + jnp.dot(
            low, onehot[...], preferred_element_type=F32
        )
        total = jnp.zeros((SHOTS, DEPTH), F32)
        for k in range(count):
            total = total + jnp.where(
                target_x == first + k, values[k * SHOTS : (k + 1) * SHOTS], 0.0
            )
        return total

    def inner_samples(moment, carry):
        samples[moment - 1] = picked(moment, HALO, ROWS - 2 * HALO)
        return carry

    lax.fori_loop(1, STEPS + 1, inner_samples, 0)

    for side, there in ((0, has_left), (1, has_right)):

        @pl.when(there)
        def _():
            for copy in halo_copies(1 - side):
                copy.wait_recv()

        @pl.when(jnp.logical_not(there))
        def _():
            slab_in[side] = jnp.zeros((7, 16, DEPTH), BF16)
            rim_in[side] = jnp.zeros((24, DEPTH), F32)

    for side in range(2):
        first = 0 if side == 0 else HALO + ROWS
        for row in range(4):
            both = slab_in[side, row].astype(F32)
            pbuf[1, first + row] = both[:SHOTS]
            qbuf[1, first + row] = both[SHOTS:]
        first = 1 if side == 0 else HALO + ROWS
        for row in range(3):
            both = slab_in[side, 4 + row].astype(F32)
            pbuf[0, first + row] = both[:SHOTS]
            qbuf[0, first + row] = both[SHOTS:]
        for k in range(6):
            coef[k, pl.ds(first + 4, 3)] = rim_in[side, pl.ds(4 * k, 3)]
        up, down = shifted(rim_in[side, pl.ds(0, 16)])
        for k in range(3):
            coef[6 + k, pl.ds(first + 4, 3)] = up[4 * k : 4 * k + 3]
            coef[9 + k, pl.ds(first + 4, 3)] = down[4 * k : 4 * k + 3]

    def outer_step(moment, carry):
        def group(side, carry):
            some_rows(moment, jnp.where(side == 0, moment, HALO + ROWS - moment), 4)
            return carry

        return lax.fori_loop(0, 2, group, carry)

    lax.fori_loop(1, STEPS + 1, outer_step, 0)

    edges = jnp.concatenate(
        [
            pbuf[moment + 1, pl.ds(first + HALO, HALO)].reshape(HALO * SHOTS, DEPTH)
            for moment in range(1, STEPS + 1)
            for first in (0, ROWS - HALO)
        ],
        axis=0,
    )
    high, low = split(edges)
    values = jnp.dot(high, onehot[...], preferred_element_type=F32) + jnp.dot(
        low, onehot[...], preferred_element_type=F32
    )
    for moment in range(STEPS):
        total = samples[moment]
        for k in range(2 * HALO):
            x = k if k < HALO else ROWS - 2 * HALO + k
            start = (moment * 2 * HALO + k) * SHOTS
            total = total + jnp.where(target_x == x, values[start : start + SHOTS], 0.0)
        samples[moment] = total

    spectra_load.wait()

    def transform(s, carry):
        drawn = [samples[moment, pl.ds(s, 1)] for moment in range(STEPS)]
        for t in range(TILES):
            lanes = pl.ds(128 * t, 128)
            value = spec[s, :, lanes]
            for moment in range(STEPS):
                value = value + table[moment] * drawn[moment][:, 128 * t : 128 * (t + 1)]
            spec[s, :, lanes] = value
            feats[core, pl.ds(s * 32, 32), lanes] = value.astype(BF16)
        return carry

    lax.fori_loop(0, SHOTS, transform, 0)

    mate = {"shot": 2 * chip + 1 - core}
    feat_copy = pltpu.make_async_remote_copy(
        src_ref=feats.at[core],
        dst_ref=feats.at[core],
        send_sem=feat_send,
        recv_sem=feat_recv,
        device_id=mate,
        device_id_type=MESH,
    )
    feat_copy.start()
    feat_copy.wait_recv()

    both = feats[...].reshape(2 * SHOTS * 32, DEPTH)
    energy[chip] = jnp.dot(
        jnp.ones((8, 2 * SHOTS * 32), BF16), both * both, preferred_element_type=F32
    )

    def energy_copy(place, owner):
        return pltpu.make_async_remote_copy(
            src_ref=energy.at[owner, pl.ds(0, 1)],
            dst_ref=energy.at[owner, pl.ds(0, 1)],
            send_sem=energy_send.at[place],
            recv_sem=energy_recv.at[owner],
            device_id={"shot": 2 * place + core},
            device_id_type=MESH,
        )

    for hop in FAR_FIRST:
        energy_copy(lax.rem(chip + hop, CHIPS), chip).start()

    def units(place):
        level = energy[place, pl.ds(0, 1)]
        inverse = jnp.where(level > 0.0, lax.rsqrt(level), 0.0)
        return level * inverse, inverse

    def in_order(row):
        straight = [row[:, 128 * k : 128 * (k + 1)] for k in range(4)]
        return [jnp.where(core == 0, straight[k], straight[(k + 1) % 4]) for k in range(4)]

    pairs = ((0, 0), (0, 1), (0, 2), (2, 2), (2, 3))
    blocks = [
        feats[:, :, pl.ds(pl.multiple_of(lax.rem(core + k, 4) * 128, 128), 128)].reshape(512, 128)
        for k in range(4)
    ]
    row_number = lax.broadcasted_iota(jnp.int32, (128, 128), 0)
    lane_number = lax.broadcasted_iota(jnp.int32, (128, 128), 1)

    def upright(row, first, count):
        here = lane_number[:count] == row_number[:count] + first
        return jnp.sum(jnp.where(here, row, 0.0), axis=1, keepdims=True)

    inverses = in_order(units(chip)[1])
    columns = {k: upright(inverses[k] * FULL, 0, 128) for k in (0, 2)}
    number = 0
    for left, right in ((0, (0, 1, 2)), (2, (2, 3))):
        product = lax.dot_general(
            blocks[left],
            jnp.concatenate([blocks[k] for k in right], axis=1),
            (((0,), (0,)), ((), ())),
            preferred_element_type=F32,
        )
        for k, block in enumerate(right):
            value = product[:, 128 * k : 128 * (k + 1)]
            half[number] = value
            part_out[number] = jnp.round(value * columns[left] * (inverses[block] * FULL)).astype(jnp.int16)
            number += 1

    def rows_of(place):
        return pl.ds(pl.multiple_of(place * CHUNK, CHUNK), CHUNK)

    def part_copy(place, owner):
        return pltpu.make_async_remote_copy(
            src_ref=part_out.at[:, rows_of(place)],
            dst_ref=part_in.at[owner],
            send_sem=part_send.at[place],
            recv_sem=part_recv.at[owner],
            device_id={"shot": 2 * place + core},
            device_id_type=MESH,
        )

    for hop in FAR_FIRST:
        part_copy(lax.rem(chip + hop, CHIPS), chip).start()

    start = chip * CHUNK
    total = [half[k, rows_of(chip)] for k in range(5)]
    for hop in NEAR_FIRST:
        place = lax.rem(chip + hop, CHIPS)
        energy_copy(place, place).wait_recv()
        roots = in_order(units(place)[0])
        columns = {k: upright(roots[k] * (1.0 / FULL), start, CHUNK) for k in (0, 2)}
        part_copy(place, place).wait_recv()
        for k, (left, right) in enumerate(pairs):
            total[k] = total[k] + part_in[place, k].astype(F32) * columns[left] * (roots[right] * (1.0 / FULL))

    level = energy[0, pl.ds(0, 1)]
    for k in range(1, CHIPS):
        level = level + energy[k, pl.ds(0, 1)]
    inverse = jnp.where(level > 0.0, lax.rsqrt(level), 0.0)
    root = level * inverse
    inverses = in_order(inverse)
    columns = {k: upright(inverses[k] * FULL, start, CHUNK) for k in (0, 2)}
    for k, (left, right) in enumerate(pairs):
        gathered[core, k, rows_of(chip)] = jnp.round(
            total[k] * columns[left] * (inverses[right] * FULL)
        ).astype(jnp.int16)

    def ring_copy(owner, place):
        return pltpu.make_async_remote_copy(
            src_ref=gathered.at[core, :, rows_of(owner)],
            dst_ref=gathered.at[core, :, rows_of(owner)],
            send_sem=ring_send.at[place],
            recv_sem=ring_recv.at[owner],
            device_id={"shot": 2 * place + core},
            device_id_type=MESH,
        )

    def pass_copy(owner, which):
        return pltpu.make_async_remote_copy(
            src_ref=gathered.at[which, :, rows_of(owner)],
            dst_ref=gathered.at[which, :, rows_of(owner)],
            send_sem=pass_send.at[owner],
            recv_sem=pass_recv.at[owner],
            device_id=mate,
            device_id_type=MESH,
        )

    for hop in FAR_FIRST:
        ring_copy(chip, lax.rem(chip + hop, CHIPS)).start()
    pass_copy(chip, core).start()

    for hop in NEAR_FIRST:
        place = lax.rem(chip + hop, CHIPS)
        ring_copy(place, place).wait_recv()
        pass_copy(place, core).start()
    for hop in (0,) + NEAR_FIRST:
        pass_copy(lax.rem(chip + hop, CHIPS), 1 - core).wait_recv()

    strips = [None] * 4
    for which in range(2):
        grid = [gathered[which, k].astype(F32) for k in range(5)]
        rows = [chosen[pl.ds(128 * (k % 4), 128)] for k in range(which, which + 4)]
        for row, left, right in (
            (which, [0.5 * grid[0], grid[1], grid[2]], rows[0:3]),
            (which + 2, [0.5 * grid[3], grid[4]], rows[2:4]),
        ):
            high, low = split(jnp.concatenate(left, axis=1))
            right = jnp.concatenate(right, axis=0)
            strips[row] = jnp.dot(high, right, preferred_element_type=F32) + jnp.dot(
                low, right, preferred_element_type=F32
            )
    strip_high, strip_low = split(jnp.concatenate(strips, axis=0))
    root_high, root_low = split(jnp.broadcast_to(root * (1.0 / FULL), (8, DEPTH)))
    chosen_root = jnp.dot(root_high, chosen[...], preferred_element_type=F32) + jnp.dot(
        root_low, chosen[...], preferred_element_type=F32
    )
    for p in range(P_MAX):
        lanes = slice(PATCH * p, PATCH * (p + 1))
        dims = (((0,), (0,)), ((), ()))
        tile = lax.dot_general(
            chosen[:, lanes], strip_high[:, lanes], dims, preferred_element_type=F32
        ) + lax.dot_general(
            chosen[:, lanes], strip_low[:, lanes], dims, preferred_element_type=F32
        )
        live = (counts_ref[0, 0] > p).astype(F32) * (1.0 / (2 * CHIPS * SHOTS * 32))
        scale = chosen_root[0:1, lanes]
        gram_ref[p] = ((tile + tile.T) * scale).T * (scale * live)

    for side, there in ((0, has_left), (1, has_right)):

        @pl.when(there)
        def _():
            for copy in halo_copies(side):
                copy.wait_send()

    feat_copy.wait_send()
    for hop in FAR_FIRST:
        place = lax.rem(chip + hop, CHIPS)
        energy_copy(place, chip).wait_send()
        part_copy(place, chip).wait_send()
        ring_copy(chip, place).wait_send()
    for hop in (0,) + NEAR_FIRST:
        pass_copy(lax.rem(chip + hop, CHIPS), core).wait_send()


def deliver(pbuf, qbuf, spec, gram, p_out, q_out, spectra_out, gram_out, sem):
    copies = [
        pltpu.make_async_copy(spec, spectra_out, sem.at[2]),
        pltpu.make_async_copy(gram, gram_out, sem.at[3]),
    ]
    for number, (source, target) in enumerate(((pbuf, p_out), (qbuf, q_out))):
        for s in range(SHOTS):
            copies.append(
                pltpu.make_async_copy(
                    source.at[STEPS + 1, pl.ds(HALO, ROWS), s], target.at[s], sem.at[number]
                )
            )
    for copy in copies:
        copy.start()
    for copy in copies:
        copy.wait()


def shards(
    bricks,
    pressure,
    auxiliary,
    pressure_prior,
    auxiliary_prior,
    courant_sq,
    thomsen_epsilon,
    thomsen_delta,
    tilt_angle,
    frequencies,
    spectra,
    target_cells,
    patch_lists,
    patch_counts,
):
    vmem = pl.BlockSpec(memory_space=pltpu.VMEM)
    smem = pl.BlockSpec(memory_space=pltpu.SMEM)
    whole = pl.BlockSpec(memory_space=pltpu.HBM)
    history = pltpu.VMEM((STEPS + 2, ROWS + 2 * HALO, SHOTS, DEPTH), F32)
    dma = pltpu.SemaphoreType.DMA
    made = pl.pallas_call(
        functools.partial(kernel, bricks),
        out_shape=(
            history,
            history,
            pltpu.VMEM((SHOTS, 32, DEPTH), F32),
            pltpu.VMEM((P_MAX, PATCH, PATCH), F32),
        ),
        in_specs=[smem, smem] + [whole] * 4 + [vmem] * 2 + [whole] * 5,
        out_specs=(vmem,) * 4,
        scratch_shapes=[
            pltpu.VMEM((4, ROWS, DEPTH), F32),
            pltpu.VMEM((12, ROWS + 16, DEPTH), F32),
            pltpu.VMEM((2, 7, 16, DEPTH), BF16),
            pltpu.VMEM((2, 7, 16, DEPTH), BF16),
            pltpu.VMEM((2, 24, DEPTH), F32),
            pltpu.VMEM((2, 24, DEPTH), F32),
            pltpu.VMEM((DEPTH, DEPTH), BF16),
            pltpu.VMEM((512, P_MAX * PATCH), BF16),
            pltpu.VMEM((STEPS, 32, 128), F32),
            pltpu.VMEM((STEPS, SHOTS, DEPTH), F32),
            pltpu.VMEM((2, SHOTS * 32, DEPTH), BF16),
            pltpu.VMEM((CHIPS, 8, DEPTH), F32),
            pltpu.VMEM((5, 128, 128), F32),
            pltpu.VMEM((5, 128, 128), jnp.int16),
            pltpu.VMEM((CHIPS, 5, CHUNK, 128), jnp.int16),
            pltpu.VMEM((2, 5, 128, 128), jnp.int16),
            dma((6,)),
            dma((2, 2)),
            dma((2, 2)),
            dma,
            dma,
            dma((CHIPS,)),
            dma((CHIPS,)),
            dma((CHIPS,)),
            dma((CHIPS,)),
            dma((CHIPS,)),
            dma((CHIPS,)),
            dma((CHIPS,)),
            dma((CHIPS,)),
        ],
        compiler_params=pltpu.CompilerParams(
            collective_id=0, has_side_effects=True, vmem_limit_bytes=50 << 20
        ),
    )(
        frequencies,
        patch_counts,
        courant_sq,
        thomsen_epsilon,
        thomsen_delta,
        tilt_angle,
        target_cells.reshape(1, -1),
        jnp.transpose(patch_lists[0], (1, 0, 2)),
        pressure,
        auxiliary,
        pressure_prior,
        auxiliary_prior,
        spectra,
    )
    field = jax.ShapeDtypeStruct((SHOTS, ROWS, DEPTH), F32)
    p_out, q_out, spectra_out, gram = pl.pallas_call(
        deliver,
        out_shape=(field, field, field, jax.ShapeDtypeStruct((P_MAX, PATCH, PATCH), F32)),
        in_specs=[vmem] * 4,
        out_specs=(whole,) * 4,
        scratch_shapes=[dma((4,))],
        compiler_params=pltpu.CompilerParams(vmem_limit_bytes=8 << 20),
    )(*(pltpu.with_memory_space_constraint(array, pltpu.VMEM) for array in made))
    return p_out, q_out, spectra_out, gram.reshape(1, 1, P_MAX, PATCH, PATCH)


def solution(mesh):
    return jax.shard_map(
        functools.partial(shards, mesh.shape["brick"]),
        mesh=mesh,
        in_specs=(
            P("shot", "brick", None),
            P("shot", "brick", None),
            P("shot", "brick", None),
            P("shot", "brick", None),
            P("brick", None),
            P("brick", None),
            P("brick", None),
            P("brick", None),
            P(),
            P("shot", None, "brick"),
            P("brick"),
            P("brick", None, None, None),
            P("brick", "shot"),
        ),
        out_specs=(
            P("shot", "brick", None),
            P("shot", "brick", None),
            P("shot", None, "brick"),
            P("brick", "shot", None, None, None),
        ),
        check_vma=False,
    )
```

```python
import functools

import jax
import jax.numpy as jnp
from jax import lax
from jax.experimental import pallas as pl
from jax.experimental.pallas import tpu as pltpu
from jax.sharding import PartitionSpec as P

STEPS = 4
PATCH = 128
P_MAX = 3
SHOTS = 8
ROWS = 32
HALO = 4
DEPTH = 512
TILES = DEPTH // 128
CHIPS = 8
CHUNK = 128 // CHIPS
RIM = (0, 2, 3, 4, 5)
FULL = 178.0
MESH = pl.DeviceIdType.MESH
F32 = jnp.float32
BF16 = jnp.bfloat16

FAR_FIRST = (4, 3, 5, 2, 6, 1, 7)
NEAR_FIRST = (1, 7, 2, 6, 3, 5, 4)


def split(value):
    high = value.astype(BF16)
    return high, (value - high.astype(F32)).astype(BF16)


def kernel(
    bricks,
    freq_in,
    counts_in,
    courant_in,
    epsilon_in,
    delta_in,
    tilt_in,
    cells_in,
    lists_in,
    p_in,
    q_in,
    pp_in,
    qq_in,
    spectra_in,
    pbuf,
    qbuf,
    spec,
    gram_ref,
    freq_ref,
    counts_ref,
    cells_ref,
    lists_ref,
    model,
    coef,
    slab_out,
    slab_in,
    rim_out,
    rim_in,
    onehot,
    chosen,
    table,
    samples,
    feats,
    energy,
    half,
    part_out,
    part_in,
    gathered,
    strips,
    word,
    in_sem,
    halo_send,
    halo_recv,
    feat_send,
    feat_recv,
    energy_send,
    energy_recv,
    part_send,
    part_recv,
    ring_send,
    ring_recv,
    pass_send,
    pass_recv,
):
    shot = lax.axis_index("shot")
    brick = lax.axis_index("brick")
    chip = shot // 2
    core = lax.rem(shot, 2)
    has_left = brick > 0
    has_right = brick < bricks - 1

    barrier = pltpu.get_barrier_semaphore()
    mate = {"shot": 2 * chip + 1 - core}
    chip_up = {"shot": 2 * lax.rem(chip + 1, CHIPS) + core}
    chip_down = {"shot": 2 * lax.rem(chip + CHIPS - 1, CHIPS) + core}
    for other in (mate, chip_up, chip_down):
        pl.semaphore_signal(barrier, inc=1, device_id=other, device_id_type=MESH)

    @pl.when(has_left)
    def _():
        pl.semaphore_signal(barrier, inc=1, device_id={"brick": brick - 1}, device_id_type=MESH)

    @pl.when(has_right)
    def _():
        pl.semaphore_signal(barrier, inc=1, device_id={"brick": brick + 1}, device_id_type=MESH)

    model_loads = [
        pltpu.make_async_copy(source, model.at[k], in_sem.at[5])
        for k, source in enumerate((courant_in, epsilon_in, delta_in, tilt_in))
    ]
    for load in model_loads:
        load.start()
    loads = []
    for number, (source, target, slot) in enumerate(
        ((p_in, pbuf, 1), (q_in, qbuf, 1), (pp_in, pbuf, 0), (qq_in, qbuf, 0))
    ):
        for s in range(SHOTS):
            loads.append(
                pltpu.make_async_copy(
                    source.at[s],
                    target.at[slot, pl.ds(HALO, ROWS), s],
                    in_sem.at[number],
                )
            )
    for load in loads:
        load.start()
    spectra_load = pltpu.make_async_copy(spectra_in, spec, in_sem.at[4])
    spectra_load.start()
    small_loads = [
        pltpu.make_async_copy(source, target, in_sem.at[6 + k])
        for k, (source, target) in enumerate(
            (
                (freq_in, freq_ref),
                (counts_in, counts_ref),
                (cells_in, cells_ref),
                (lists_in, lists_ref),
            )
        )
    ]
    for load in small_loads:
        load.start()

    def shifted(value):
        lane = lax.broadcasted_iota(jnp.int32, value.shape, 1)
        return (
            jnp.where(lane == 0, 0.0, pltpu.roll(value, 1, 1)),
            jnp.where(lane == DEPTH - 1, 0.0, pltpu.roll(value, DEPTH - 1, 1)),
        )

    for load in model_loads:
        load.wait()
    sine = jnp.sin(model[3])
    cosine = jnp.cos(model[3])
    courant = model[0]
    own = pl.ds(8, ROWS)
    turns = (cosine * cosine, sine * sine, 0.5 * sine * cosine)
    for k, value in enumerate(turns):
        coef[k, own] = value
        coef[6 + k, own], coef[9 + k, own] = shifted(value)
    coef[3, own] = courant
    coef[4, own] = courant * (1.0 + 2.0 * model[1])
    coef[5, own] = courant * (1.0 + 2.0 * model[2])
    for side, first in ((0, 8), (1, 8 + ROWS - 3)):
        rim_out[side] = jnp.concatenate(
            [coef[k, pl.ds(first, 3)] for k in RIM] + [jnp.zeros((1, DEPTH), F32)], axis=0
        ).astype(BF16)
    for load in loads:
        load.wait()
    for side in range(2):
        first = HALO if side == 0 else HALO + ROWS - 4
        for row in range(4):
            slab_out[side, row] = jnp.concatenate(
                [pbuf[1, first + row], qbuf[1, first + row]], axis=0
            ).astype(BF16)
        first = HALO if side == 0 else HALO + ROWS - 3
        for row in range(3):
            slab_out[side, 4 + row] = jnp.concatenate(
                [pbuf[0, first + row], qbuf[0, first + row]], axis=0
            ).astype(BF16)

    pl.semaphore_wait(
        barrier, 3 + has_left.astype(jnp.int32) + has_right.astype(jnp.int32)
    )

    def spread(j):
        pl.semaphore_signal(word.at[j, 0], inc=1, device_id=chip_up, device_id_type=MESH)
        pl.semaphore_signal(word.at[j, 1], inc=1, device_id=chip_down, device_id_type=MESH)

    def hear(j):
        pl.semaphore_wait(word.at[j, 0], 1)
        pl.semaphore_wait(word.at[j, 1], 1)

    spread(0)

    def halo_copies(side):
        target = {"brick": brick - 1 if side == 0 else brick + 1}
        return [
            pltpu.make_async_remote_copy(
                src_ref=slab_out.at[side],
                dst_ref=slab_in.at[1 - side],
                send_sem=halo_send.at[side, 0],
                recv_sem=halo_recv.at[1 - side, 0],
                device_id=target,
                device_id_type=MESH,
            ),
            pltpu.make_async_remote_copy(
                src_ref=rim_out.at[side],
                dst_ref=rim_in.at[1 - side],
                send_sem=halo_send.at[side, 1],
                recv_sem=halo_recv.at[1 - side, 1],
                device_id=target,
                device_id_type=MESH,
            ),
        ]

    for side, there in ((0, has_left), (1, has_right)):

        @pl.when(there)
        def _():
            for copy in halo_copies(side):
                copy.start()

    for load in small_loads:
        load.wait()
    cells = cells_ref[...]
    target_x = cells >> 9
    target_z = cells & (DEPTH - 1)
    onehot[...] = (
        lax.broadcasted_iota(jnp.int32, (DEPTH, DEPTH), 0) == target_z
    ).astype(F32).astype(BF16)

    for p in range(P_MAX):
        chosen[:, pl.ds(PATCH * p, PATCH)] = (
            (lax.broadcasted_iota(jnp.int32, (512, PATCH), 0) == lists_ref[p, pl.ds(shot, 1)])
            .astype(F32)
            .astype(BF16)
        )

    number = lax.broadcasted_iota(jnp.int32, (16, 128), 0)
    frequency = jnp.zeros((16, 128), F32)
    for k in range(16):
        frequency = jnp.where(number == k, freq_ref[k], frequency)
    for moment in range(STEPS):
        angle = frequency * (moment + 1.0)
        table[moment, pl.ds(0, 16)] = jnp.cos(angle)
        table[moment, pl.ds(16, 16)] = -jnp.sin(angle)

    lane = lax.broadcasted_iota(jnp.int32, (SHOTS, 128), 1)
    first_lane = lane == 0
    last_lane = lane == 127

    def tiles(value):
        return [value[:, 128 * k : 128 * (k + 1)] for k in range(TILES)]

    def deeper(value):
        turned = [pltpu.roll(tile, 127, 1) for tile in value]
        return [jnp.where(last_lane, turned[(k + 1) % TILES], turned[k]) for k in range(TILES)]

    def shallower(value):
        turned = [pltpu.roll(tile, 1, 1) for tile in value]
        return [jnp.where(first_lane, turned[k - 1], turned[k]) for k in range(TILES)]

    def mix(first, a, second, b, sign):
        if sign > 0:
            return [w * x + v * y for w, x, v, y in zip(first, a, second, b)]
        return [w * x - v * y for w, x, v, y in zip(first, a, second, b)]

    def some_rows(moment, row, count):
        p_rows = [tiles(pbuf[moment, row + k]) for k in range(-1, count + 1)]
        q_rows = [tiles(qbuf[moment, row + k]) for k in range(-1, count + 1)]
        for k in range(count):
            at = row + k
            (
                cos_sq,
                sin_sq,
                speed,
                speed_e,
                speed_d,
                cos_up,
                sin_up,
                twist_up,
                cos_down,
                sin_down,
                twist_down,
            ) = (
                tiles(jnp.broadcast_to(coef[number, pl.ds(at + 4, 1)], (SHOTS, DEPTH)))
                for number in (0, 1, 3, 4, 5, 6, 7, 8, 9, 10, 11)
            )
            p_steep = [a + b for a, b in zip(p_rows[k], p_rows[k + 2])]
            p_slope = [b - a for a, b in zip(p_rows[k], p_rows[k + 2])]
            q_steep = [a + b for a, b in zip(q_rows[k], q_rows[k + 2])]
            q_slope = [b - a for a, b in zip(q_rows[k], q_rows[k + 2])]
            p_deeper = deeper(mix(sin_up, p_rows[k + 1], twist_up, p_slope, -1))
            p_shallower = shallower(mix(sin_down, p_rows[k + 1], twist_down, p_slope, 1))
            q_deeper = deeper(mix(cos_up, q_rows[k + 1], twist_up, q_slope, 1))
            q_shallower = shallower(mix(cos_down, q_rows[k + 1], twist_down, q_slope, -1))
            p_old = tiles(pbuf[moment - 1, at])
            q_old = tiles(qbuf[moment - 1, at])
            for t in range(TILES):
                p_two = p_rows[k + 1][t] + p_rows[k + 1][t]
                q_two = q_rows[k + 1][t] + q_rows[k + 1][t]
                across = (cos_sq[t] * p_steep[t] - p_two) + (p_deeper[t] + p_shallower[t])
                along = (sin_sq[t] * q_steep[t] - q_two) + (q_deeper[t] + q_shallower[t])
                push = speed[t] * along
                lanes = pl.ds(128 * t, 128)
                pbuf[moment + 1, at, :, lanes] = (p_two - p_old[t]) + (speed_e[t] * across + push)
                qbuf[moment + 1, at, :, lanes] = (q_two - q_old[t]) + (speed_d[t] * across + push)

    def inner_step(moment, carry):
        def group(number, carry):
            some_rows(moment, moment + HALO + 4 * number, 4)
            return carry

        return lax.fori_loop(0, (ROWS - 2 * moment + 3) // 4, group, carry)

    lax.fori_loop(1, STEPS + 1, inner_step, 0)
    hear(0)
    spread(1)

    def picked(moment, first, count):
        rows = pbuf[moment + 1, pl.ds(first + HALO, count)].reshape(count * SHOTS, DEPTH)
        high, low = split(rows)
        values = jnp.dot(high, onehot[...], preferred_element_type=F32) + jnp.dot(
            low, onehot[...], preferred_element_type=F32
        )
        total = jnp.zeros((SHOTS, DEPTH), F32)
        for k in range(count):
            total = total + jnp.where(
                target_x == first + k, values[k * SHOTS : (k + 1) * SHOTS], 0.0
            )
        return total

    def inner_samples(moment, carry):
        samples[moment - 1] = picked(moment, HALO, ROWS - 2 * HALO)
        return carry

    lax.fori_loop(1, STEPS + 1, inner_samples, 0)
    hear(1)
    spread(2)

    for side, there in ((0, has_left), (1, has_right)):

        @pl.when(there)
        def _():
            for copy in halo_copies(1 - side):
                copy.wait_recv()

        @pl.when(jnp.logical_not(there))
        def _():
            slab_in[side] = jnp.zeros((7, 16, DEPTH), BF16)
            rim_in[side] = jnp.zeros((16, DEPTH), BF16)

    for side in range(2):
        first = 0 if side == 0 else HALO + ROWS
        for row in range(4):
            both = slab_in[side, row].astype(F32)
            pbuf[1, first + row] = both[:SHOTS]
            qbuf[1, first + row] = both[SHOTS:]
        first = 1 if side == 0 else HALO + ROWS
        for row in range(3):
            both = slab_in[side, 4 + row].astype(F32)
            pbuf[0, first + row] = both[:SHOTS]
            qbuf[0, first + row] = both[SHOTS:]
        rim = rim_in[side].astype(F32)
        for k, number in enumerate(RIM):
            coef[number, pl.ds(first + 4, 3)] = rim[3 * k : 3 * k + 3]
        coef[1, pl.ds(first + 4, 3)] = 1.0 - rim[:3]
        turns_up, turns_down = shifted(rim[:8])
        rest_up, rest_down = shifted(1.0 - rim[:8])
        for number, value, start in (
            (6, turns_up, 0),
            (7, rest_up, 0),
            (8, turns_up, 3),
            (9, turns_down, 0),
            (10, rest_down, 0),
            (11, turns_down, 3),
        ):
            coef[number, pl.ds(first + 4, 3)] = value[start : start + 3]

    def outer_step(moment, carry):
        def group(side, carry):
            some_rows(moment, jnp.where(side == 0, moment, HALO + ROWS - moment), 4)
            return carry

        return lax.fori_loop(0, 2, group, carry)

    lax.fori_loop(1, STEPS + 1, outer_step, 0)

    edges = jnp.concatenate(
        [
            pbuf[moment + 1, pl.ds(first + HALO, HALO)].reshape(HALO * SHOTS, DEPTH)
            for moment in range(1, STEPS + 1)
            for first in (0, ROWS - HALO)
        ],
        axis=0,
    )
    high, low = split(edges)
    values = jnp.dot(high, onehot[...], preferred_element_type=F32) + jnp.dot(
        low, onehot[...], preferred_element_type=F32
    )
    for moment in range(STEPS):
        total = samples[moment]
        for k in range(2 * HALO):
            x = k if k < HALO else ROWS - 2 * HALO + k
            start = (moment * 2 * HALO + k) * SHOTS
            total = total + jnp.where(target_x == x, values[start : start + SHOTS], 0.0)
        samples[moment] = total

    spectra_load.wait()

    def transform(s, carry):
        drawn = [samples[moment, pl.ds(s, 1)] for moment in range(STEPS)]
        for t in range(TILES):
            lanes = pl.ds(128 * t, 128)
            value = spec[s, :, lanes]
            for moment in range(STEPS):
                value = value + table[moment] * drawn[moment][:, 128 * t : 128 * (t + 1)]
            spec[s, :, lanes] = value
            feats[core, pl.ds(s * 32, 32), lanes] = value.astype(BF16)
        return carry

    lax.fori_loop(0, SHOTS, transform, 0)

    feat_copy = pltpu.make_async_remote_copy(
        src_ref=feats.at[core],
        dst_ref=feats.at[core],
        send_sem=feat_send,
        recv_sem=feat_recv,
        device_id=mate,
        device_id_type=MESH,
    )
    feat_copy.start()
    feat_copy.wait_recv()

    both = feats[...].reshape(2 * SHOTS * 32, DEPTH)
    energy[chip] = jnp.dot(
        jnp.ones((8, 2 * SHOTS * 32), BF16), both * both, preferred_element_type=F32
    )

    def energy_copy(place, owner):
        return pltpu.make_async_remote_copy(
            src_ref=energy.at[owner, pl.ds(0, 1)],
            dst_ref=energy.at[owner, pl.ds(0, 1)],
            send_sem=energy_send.at[place],
            recv_sem=energy_recv.at[owner],
            device_id={"shot": 2 * place + core},
            device_id_type=MESH,
        )

    hear(2)
    for hop in FAR_FIRST:
        energy_copy(lax.rem(chip + hop, CHIPS), chip).start()

    def units(place):
        level = energy[place, pl.ds(0, 1)]
        inverse = jnp.where(level > 0.0, lax.rsqrt(level), 0.0)
        return level * inverse, inverse

    def in_order(row):
        straight = [row[:, 128 * k : 128 * (k + 1)] for k in range(4)]
        return [jnp.where(core == 0, straight[k], straight[(k + 1) % 4]) for k in range(4)]

    pairs = ((0, 0), (0, 1), (0, 2), (2, 2), (2, 3))
    blocks = [
        feats[:, :, pl.ds(pl.multiple_of(lax.rem(core + k, 4) * 128, 128), 128)].reshape(512, 128)
        for k in range(4)
    ]
    row_number = lax.broadcasted_iota(jnp.int32, (128, 128), 0)
    lane_number = lax.broadcasted_iota(jnp.int32, (128, 128), 1)

    def upright(row, first, count):
        here = lane_number[:count] == row_number[:count] + first
        return jnp.sum(jnp.where(here, row, 0.0), axis=1, keepdims=True)

    inverses = in_order(units(chip)[1])
    columns = {k: upright(inverses[k] * FULL, 0, 128) for k in (0, 2)}
    number = 0
    for left, right in ((0, (0, 1, 2)), (2, (2, 3))):
        product = lax.dot_general(
            blocks[left],
            jnp.concatenate([blocks[k] for k in right], axis=1),
            (((0,), (0,)), ((), ())),
            preferred_element_type=F32,
        )
        for k, block in enumerate(right):
            value = product[:, 128 * k : 128 * (k + 1)]
            half[number] = value
            part_out[number] = jnp.round(value * columns[left] * (inverses[block] * FULL)).astype(jnp.int16)
            number += 1

    def rows_of(place):
        return pl.ds(pl.multiple_of(place * CHUNK, CHUNK), CHUNK)

    def part_copy(place, owner):
        return pltpu.make_async_remote_copy(
            src_ref=part_out.at[:, rows_of(place)],
            dst_ref=part_in.at[owner],
            send_sem=part_send.at[place],
            recv_sem=part_recv.at[owner],
            device_id={"shot": 2 * place + core},
            device_id_type=MESH,
        )

    for hop in FAR_FIRST:
        part_copy(lax.rem(chip + hop, CHIPS), chip).start()

    start = chip * CHUNK
    total = [half[k, rows_of(chip)] for k in range(5)]
    for hop in NEAR_FIRST:
        place = lax.rem(chip + hop, CHIPS)
        energy_copy(place, place).wait_recv()
        roots = in_order(units(place)[0])
        columns = {k: upright(roots[k] * (1.0 / FULL), start, CHUNK) for k in (0, 2)}
        part_copy(place, place).wait_recv()
        for k, (left, right) in enumerate(pairs):
            total[k] = total[k] + part_in[place, k].astype(F32) * columns[left] * (roots[right] * (1.0 / FULL))

    level = energy[0, pl.ds(0, 1)]
    for k in range(1, CHIPS):
        level = level + energy[k, pl.ds(0, 1)]
    inverse = jnp.where(level > 0.0, lax.rsqrt(level), 0.0)
    root = level * inverse
    inverses = in_order(inverse)
    columns = {k: upright(inverses[k] * FULL, start, CHUNK) for k in (0, 2)}
    for k, (left, right) in enumerate(pairs):
        gathered[core, k, rows_of(chip)] = jnp.round(
            total[k] * columns[left] * (inverses[right] * FULL)
        ).astype(jnp.int16)

    def ring_copy(owner, place):
        return pltpu.make_async_remote_copy(
            src_ref=gathered.at[core, :, rows_of(owner)],
            dst_ref=gathered.at[core, :, rows_of(owner)],
            send_sem=ring_send.at[place],
            recv_sem=ring_recv.at[owner],
            device_id={"shot": 2 * place + core},
            device_id_type=MESH,
        )

    def pass_copy(owner, which):
        return pltpu.make_async_remote_copy(
            src_ref=gathered.at[which, :, rows_of(owner)],
            dst_ref=gathered.at[which, :, rows_of(owner)],
            send_sem=pass_send.at[owner],
            recv_sem=pass_recv.at[owner],
            device_id=mate,
            device_id_type=MESH,
        )

    for hop in FAR_FIRST:
        ring_copy(chip, lax.rem(chip + hop, CHIPS)).start()
    pass_copy(chip, core).start()

    for hop in NEAR_FIRST:
        place = lax.rem(chip + hop, CHIPS)
        ring_copy(place, place).wait_recv()
        pass_copy(place, core).start()
    def strips_of(which):
        grid = [gathered[which, k].astype(F32) for k in range(5)]

        def picks(first, count):
            return [
                chosen[pl.ds(pl.multiple_of(lax.rem(which + k, 4) * 128, 128), 128)]
                for k in range(first, first + count)
            ]

        for row, left, right in (
            (0, [0.5 * grid[0], grid[1], grid[2]], picks(0, 3)),
            (2, [0.5 * grid[3], grid[4]], picks(2, 2)),
        ):
            high, low = split(jnp.concatenate(left, axis=1))
            right = jnp.concatenate(right, axis=0)
            strips[which + row] = jnp.dot(high, right, preferred_element_type=F32) + jnp.dot(
                low, right, preferred_element_type=F32
            )

    strips_of(core)
    for hop in (0,) + NEAR_FIRST:
        pass_copy(lax.rem(chip + hop, CHIPS), 1 - core).wait_recv()
    strips_of(1 - core)
    strip_high, strip_low = split(strips[...].reshape(512, P_MAX * PATCH))
    root_high, root_low = split(jnp.broadcast_to(root * (1.0 / FULL), (8, DEPTH)))
    chosen_root = jnp.dot(root_high, chosen[...], preferred_element_type=F32) + jnp.dot(
        root_low, chosen[...], preferred_element_type=F32
    )
    for p in range(P_MAX):
        lanes = slice(PATCH * p, PATCH * (p + 1))
        dims = (((0,), (0,)), ((), ()))
        tile = lax.dot_general(
            chosen[:, lanes], strip_high[:, lanes], dims, preferred_element_type=F32
        ) + lax.dot_general(
            chosen[:, lanes], strip_low[:, lanes], dims, preferred_element_type=F32
        )
        live = (counts_ref[0, 0] > p).astype(F32) * (1.0 / (2 * CHIPS * SHOTS * 32))
        scale = chosen_root[0:1, lanes]
        gram_ref[p] = ((tile + tile.T) * scale).T * (scale * live)

    for side, there in ((0, has_left), (1, has_right)):

        @pl.when(there)
        def _():
            for copy in halo_copies(side):
                copy.wait_send()

    feat_copy.wait_send()
    for hop in FAR_FIRST:
        place = lax.rem(chip + hop, CHIPS)
        energy_copy(place, chip).wait_send()
        part_copy(place, chip).wait_send()
        ring_copy(chip, place).wait_send()
    for hop in (0,) + NEAR_FIRST:
        pass_copy(lax.rem(chip + hop, CHIPS), core).wait_send()


def deliver(pbuf, qbuf, spec, gram, p_out, q_out, spectra_out, gram_out, sem):
    copies = [
        pltpu.make_async_copy(spec, spectra_out, sem.at[2]),
        pltpu.make_async_copy(gram, gram_out, sem.at[3]),
    ]
    for number, (source, target) in enumerate(((pbuf, p_out), (qbuf, q_out))):
        for s in range(SHOTS):
            copies.append(
                pltpu.make_async_copy(
                    source.at[STEPS + 1, pl.ds(HALO, ROWS), s], target.at[s], sem.at[number]
                )
            )
    for copy in copies:
        copy.start()
    for copy in copies:
        copy.wait()


def shards(
    bricks,
    pressure,
    auxiliary,
    pressure_prior,
    auxiliary_prior,
    courant_sq,
    thomsen_epsilon,
    thomsen_delta,
    tilt_angle,
    frequencies,
    spectra,
    target_cells,
    patch_lists,
    patch_counts,
):
    vmem = pl.BlockSpec(memory_space=pltpu.VMEM)
    whole = pl.BlockSpec(memory_space=pltpu.HBM)
    history = pltpu.VMEM((STEPS + 2, ROWS + 2 * HALO, SHOTS, DEPTH), F32)
    dma = pltpu.SemaphoreType.DMA
    made = pl.pallas_call(
        functools.partial(kernel, bricks),
        out_shape=(
            history,
            history,
            pltpu.VMEM((SHOTS, 32, DEPTH), F32),
            pltpu.VMEM((P_MAX, PATCH, PATCH), F32),
        ),
        in_specs=[whole] * 13,
        out_specs=(vmem,) * 4,
        scratch_shapes=[
            pltpu.SMEM((16,), F32),
            pltpu.SMEM((1, 1), jnp.int32),
            pltpu.VMEM((1, DEPTH), jnp.int32),
            pltpu.VMEM((P_MAX, 2 * CHIPS, PATCH), jnp.int32),
            pltpu.VMEM((4, ROWS, DEPTH), F32),
            pltpu.VMEM((12, ROWS + 16, DEPTH), F32),
            pltpu.VMEM((2, 7, 16, DEPTH), BF16),
            pltpu.VMEM((2, 7, 16, DEPTH), BF16),
            pltpu.VMEM((2, 16, DEPTH), BF16),
            pltpu.VMEM((2, 16, DEPTH), BF16),
            pltpu.VMEM((DEPTH, DEPTH), BF16),
            pltpu.VMEM((512, P_MAX * PATCH), BF16),
            pltpu.VMEM((STEPS, 32, 128), F32),
            pltpu.VMEM((STEPS, SHOTS, DEPTH), F32),
            pltpu.VMEM((2, SHOTS * 32, DEPTH), BF16),
            pltpu.VMEM((CHIPS, 8, DEPTH), F32),
            pltpu.VMEM((5, 128, 128), F32),
            pltpu.VMEM((5, 128, 128), jnp.int16),
            pltpu.VMEM((CHIPS, 5, CHUNK, 128), jnp.int16),
            pltpu.VMEM((2, 5, 128, 128), jnp.int16),
            pltpu.VMEM((4, 128, P_MAX * PATCH), F32),
            pltpu.SemaphoreType.REGULAR((3, 2)),
            dma((10,)),
            dma((2, 2)),
            dma((2, 2)),
            dma,
            dma,
            dma((CHIPS,)),
            dma((CHIPS,)),
            dma((CHIPS,)),
            dma((CHIPS,)),
            dma((CHIPS,)),
            dma((CHIPS,)),
            dma((CHIPS,)),
            dma((CHIPS,)),
        ],
        compiler_params=pltpu.CompilerParams(
            collective_id=0, has_side_effects=True, vmem_limit_bytes=50 << 20
        ),
    )(
        frequencies,
        patch_counts,
        courant_sq,
        thomsen_epsilon,
        thomsen_delta,
        tilt_angle,
        target_cells.reshape(1, -1),
        jnp.transpose(patch_lists[0], (1, 0, 2)),
        pressure,
        auxiliary,
        pressure_prior,
        auxiliary_prior,
        spectra,
    )
    field = jax.ShapeDtypeStruct((SHOTS, ROWS, DEPTH), F32)
    p_out, q_out, spectra_out, gram = pl.pallas_call(
        deliver,
        out_shape=(field, field, field, jax.ShapeDtypeStruct((P_MAX, PATCH, PATCH), F32)),
        in_specs=[vmem] * 4,
        out_specs=(whole,) * 4,
        scratch_shapes=[dma((4,))],
        compiler_params=pltpu.CompilerParams(vmem_limit_bytes=8 << 20),
    )(*(pltpu.with_memory_space_constraint(array, pltpu.VMEM) for array in made))
    return p_out, q_out, spectra_out, gram.reshape(1, 1, P_MAX, PATCH, PATCH)


def solution(mesh):
    return jax.shard_map(
        functools.partial(shards, mesh.shape["brick"]),
        mesh=mesh,
        in_specs=(
            P("shot", "brick", None),
            P("shot", "brick", None),
            P("shot", "brick", None),
            P("shot", "brick", None),
            P("brick", None),
            P("brick", None),
            P("brick", None),
            P("brick", None),
            P(),
            P("shot", None, "brick"),
            P("brick"),
            P("brick", None, None, None),
            P("brick", "shot"),
        ),
        out_specs=(
            P("shot", "brick", None),
            P("shot", "brick", None),
            P("shot", None, "brick"),
            P("brick", "shot", None, None, None),
        ),
        check_vma=False,
    )
```

```python
import functools

import jax
import jax.numpy as jnp
from jax import lax
from jax.experimental import pallas as pl
from jax.experimental.pallas import tpu as pltpu
from jax.sharding import PartitionSpec as P

STEPS = 4
PATCH = 128
P_MAX = 3
SHOTS = 8
ROWS = 32
HALO = 4
DEPTH = 512
TILES = DEPTH // 128
CHIPS = 8
CHUNK = 128 // CHIPS
RIM = (0, 2, 3, 4, 5)
FULL = 178.0
MESH = pl.DeviceIdType.MESH
F32 = jnp.float32
BF16 = jnp.bfloat16

FAR_FIRST = (4, 3, 5, 2, 6, 1, 7)
NEAR_FIRST = (1, 7, 2, 6, 3, 5, 4)


def split(value):
    high = value.astype(BF16)
    return high, (value - high.astype(F32)).astype(BF16)


def kernel(
    bricks,
    freq_in,
    counts_in,
    courant_in,
    epsilon_in,
    delta_in,
    tilt_in,
    cells_in,
    lists_in,
    p_in,
    q_in,
    pp_in,
    qq_in,
    spectra_in,
    pbuf,
    qbuf,
    spec,
    gram_ref,
    freq_ref,
    counts_ref,
    cells_ref,
    lists_ref,
    model,
    coef,
    slab_out,
    slab_in,
    rim_out,
    rim_in,
    onehot,
    chosen,
    table,
    samples,
    feats,
    energy,
    half,
    part_out,
    part_in,
    gathered,
    strips,
    word,
    in_sem,
    halo_send,
    halo_recv,
    feat_send,
    feat_recv,
    energy_send,
    energy_recv,
    part_send,
    part_recv,
    ring_send,
    ring_recv,
    pass_send,
    pass_recv,
):
    shot = lax.axis_index("shot")
    brick = lax.axis_index("brick")
    chip = shot // 2
    core = lax.rem(shot, 2)
    has_left = brick > 0
    has_right = brick < bricks - 1

    barrier = pltpu.get_barrier_semaphore()
    mate = {"shot": 2 * chip + 1 - core}
    chip_up = {"shot": 2 * lax.rem(chip + 1, CHIPS) + core}
    chip_down = {"shot": 2 * lax.rem(chip + CHIPS - 1, CHIPS) + core}
    for other in (mate, chip_up, chip_down):
        pl.semaphore_signal(barrier, inc=1, device_id=other, device_id_type=MESH)

    @pl.when(has_left)
    def _():
        pl.semaphore_signal(barrier, inc=1, device_id={"brick": brick - 1}, device_id_type=MESH)

    @pl.when(has_right)
    def _():
        pl.semaphore_signal(barrier, inc=1, device_id={"brick": brick + 1}, device_id_type=MESH)

    model_loads = [
        pltpu.make_async_copy(source, model.at[k], in_sem.at[5])
        for k, source in enumerate((courant_in, epsilon_in, delta_in, tilt_in))
    ]
    for load in model_loads:
        load.start()
    loads = []
    for number, (source, target, slot) in enumerate(
        ((p_in, pbuf, 1), (q_in, qbuf, 1), (pp_in, pbuf, 0), (qq_in, qbuf, 0))
    ):
        for s in range(SHOTS):
            loads.append(
                pltpu.make_async_copy(
                    source.at[s],
                    target.at[slot, pl.ds(HALO, ROWS), s],
                    in_sem.at[number],
                )
            )
    for load in loads:
        load.start()
    spectra_load = pltpu.make_async_copy(spectra_in, spec, in_sem.at[4])
    spectra_load.start()
    small_loads = [
        pltpu.make_async_copy(source, target, in_sem.at[6 + k])
        for k, (source, target) in enumerate(
            (
                (freq_in, freq_ref),
                (counts_in, counts_ref),
                (cells_in, cells_ref),
                (lists_in, lists_ref),
            )
        )
    ]
    for load in small_loads:
        load.start()

    def shifted(value):
        lane = lax.broadcasted_iota(jnp.int32, value.shape, 1)
        return (
            jnp.where(lane == 0, 0.0, pltpu.roll(value, 1, 1)),
            jnp.where(lane == DEPTH - 1, 0.0, pltpu.roll(value, DEPTH - 1, 1)),
        )

    for load in model_loads:
        load.wait()
    sine = jnp.sin(model[3])
    cosine = jnp.cos(model[3])
    courant = model[0]
    own = pl.ds(8, ROWS)
    turns = (cosine * cosine, sine * sine, 0.5 * sine * cosine)
    for k, value in enumerate(turns):
        coef[k, own] = value
        coef[6 + k, own], coef[9 + k, own] = shifted(value)
    coef[3, own] = courant
    coef[4, own] = courant * (1.0 + 2.0 * model[1])
    coef[5, own] = courant * (1.0 + 2.0 * model[2])
    for side, first in ((0, 8), (1, 8 + ROWS - 3)):
        rim_out[side] = jnp.concatenate(
            [coef[k, pl.ds(first, 3)] for k in RIM] + [jnp.zeros((1, DEPTH), F32)], axis=0
        ).astype(BF16)
    for load in loads:
        load.wait()
    lane = lax.broadcasted_iota(jnp.int32, (SHOTS, 128), 1)
    first_lane = lane == 0
    last_lane = lane == 127

    def tiles(value):
        return [value[:, 128 * k : 128 * (k + 1)] for k in range(TILES)]

    def deeper(value):
        turned = [pltpu.roll(tile, 127, 1) for tile in value]
        return [jnp.where(last_lane, turned[(k + 1) % TILES], turned[k]) for k in range(TILES)]

    def shallower(value):
        turned = [pltpu.roll(tile, 1, 1) for tile in value]
        return [jnp.where(first_lane, turned[k - 1], turned[k]) for k in range(TILES)]

    def mix(first, a, second, b, sign):
        if sign > 0:
            return [w * x + v * y for w, x, v, y in zip(first, a, second, b)]
        return [w * x - v * y for w, x, v, y in zip(first, a, second, b)]

    def some_rows(moment, row, count):
        p_rows = [tiles(pbuf[moment, row + k]) for k in range(-1, count + 1)]
        q_rows = [tiles(qbuf[moment, row + k]) for k in range(-1, count + 1)]
        for k in range(count):
            at = row + k
            (
                cos_sq,
                sin_sq,
                speed,
                speed_e,
                speed_d,
                cos_up,
                sin_up,
                twist_up,
                cos_down,
                sin_down,
                twist_down,
            ) = (
                tiles(jnp.broadcast_to(coef[number, pl.ds(at + 4, 1)], (SHOTS, DEPTH)))
                for number in (0, 1, 3, 4, 5, 6, 7, 8, 9, 10, 11)
            )
            p_steep = [a + b for a, b in zip(p_rows[k], p_rows[k + 2])]
            p_slope = [b - a for a, b in zip(p_rows[k], p_rows[k + 2])]
            q_steep = [a + b for a, b in zip(q_rows[k], q_rows[k + 2])]
            q_slope = [b - a for a, b in zip(q_rows[k], q_rows[k + 2])]
            p_deeper = deeper(mix(sin_up, p_rows[k + 1], twist_up, p_slope, -1))
            p_shallower = shallower(mix(sin_down, p_rows[k + 1], twist_down, p_slope, 1))
            q_deeper = deeper(mix(cos_up, q_rows[k + 1], twist_up, q_slope, 1))
            q_shallower = shallower(mix(cos_down, q_rows[k + 1], twist_down, q_slope, -1))
            p_old = tiles(pbuf[moment - 1, at])
            q_old = tiles(qbuf[moment - 1, at])
            for t in range(TILES):
                p_two = p_rows[k + 1][t] + p_rows[k + 1][t]
                q_two = q_rows[k + 1][t] + q_rows[k + 1][t]
                across = (cos_sq[t] * p_steep[t] - p_two) + (p_deeper[t] + p_shallower[t])
                along = (sin_sq[t] * q_steep[t] - q_two) + (q_deeper[t] + q_shallower[t])
                push = speed[t] * along
                lanes = pl.ds(128 * t, 128)
                pbuf[moment + 1, at, :, lanes] = (p_two - p_old[t]) + (speed_e[t] * across + push)
                qbuf[moment + 1, at, :, lanes] = (q_two - q_old[t]) + (speed_d[t] * across + push)

    some_rows(1, HALO + 1, 2)
    some_rows(1, HALO + ROWS - 3, 2)

    sent = (((1, 0), (1, 1), (0, 0), (2, 1), (2, 2)), ((1, 31), (1, 30), (0, 31), (2, 30), (2, 29)))
    for side in range(2):
        for k, (time, x) in enumerate(sent[side]):
            slab_out[side, k] = jnp.concatenate(
                [pbuf[time, HALO + x], qbuf[time, HALO + x]], axis=0
            ).astype(BF16)

    pl.semaphore_wait(
        barrier, 3 + has_left.astype(jnp.int32) + has_right.astype(jnp.int32)
    )

    def spread(j):
        pl.semaphore_signal(word.at[j, 0], inc=1, device_id=chip_up, device_id_type=MESH)
        pl.semaphore_signal(word.at[j, 1], inc=1, device_id=chip_down, device_id_type=MESH)

    def hear(j):
        pl.semaphore_wait(word.at[j, 0], 1)
        pl.semaphore_wait(word.at[j, 1], 1)

    spread(0)

    def halo_copies(side):
        target = {"brick": brick - 1 if side == 0 else brick + 1}
        return [
            pltpu.make_async_remote_copy(
                src_ref=slab_out.at[side],
                dst_ref=slab_in.at[1 - side],
                send_sem=halo_send.at[side, 0],
                recv_sem=halo_recv.at[1 - side, 0],
                device_id=target,
                device_id_type=MESH,
            ),
            pltpu.make_async_remote_copy(
                src_ref=rim_out.at[side],
                dst_ref=rim_in.at[1 - side],
                send_sem=halo_send.at[side, 1],
                recv_sem=halo_recv.at[1 - side, 1],
                device_id=target,
                device_id_type=MESH,
            ),
        ]

    for side, there in ((0, has_left), (1, has_right)):

        @pl.when(there)
        def _():
            for copy in halo_copies(side):
                copy.start()

    for load in small_loads:
        load.wait()
    cells = cells_ref[...]
    target_x = cells >> 9
    target_z = cells & (DEPTH - 1)
    onehot[...] = (
        lax.broadcasted_iota(jnp.int32, (DEPTH, DEPTH), 0) == target_z
    ).astype(F32).astype(BF16)

    for p in range(P_MAX):
        chosen[:, pl.ds(PATCH * p, PATCH)] = (
            (lax.broadcasted_iota(jnp.int32, (512, PATCH), 0) == lists_ref[p, pl.ds(shot, 1)])
            .astype(F32)
            .astype(BF16)
        )

    number = lax.broadcasted_iota(jnp.int32, (16, 128), 0)
    frequency = jnp.zeros((16, 128), F32)
    for k in range(16):
        frequency = jnp.where(number == k, freq_ref[k], frequency)
    for moment in range(STEPS):
        angle = frequency * (moment + 1.0)
        table[moment, pl.ds(0, 16)] = jnp.cos(angle)
        table[moment, pl.ds(16, 16)] = -jnp.sin(angle)

    def inner_step(moment, carry):
        def group(number, carry):
            some_rows(moment, moment + HALO + 4 * number, 4)
            return carry

        return lax.fori_loop(0, (ROWS - 2 * moment + 3) // 4, group, carry)

    lax.fori_loop(1, STEPS + 1, inner_step, 0)
    hear(0)
    spread(1)

    def picked(moment, first, count):
        rows = pbuf[moment + 1, pl.ds(first + HALO, count)].reshape(count * SHOTS, DEPTH)
        high, low = split(rows)
        values = jnp.dot(high, onehot[...], preferred_element_type=F32) + jnp.dot(
            low, onehot[...], preferred_element_type=F32
        )
        total = jnp.zeros((SHOTS, DEPTH), F32)
        for k in range(count):
            total = total + jnp.where(
                target_x == first + k, values[k * SHOTS : (k + 1) * SHOTS], 0.0
            )
        return total

    def inner_samples(moment, carry):
        samples[moment - 1] = picked(moment, HALO, ROWS - 2 * HALO)
        return carry

    lax.fori_loop(1, STEPS + 1, inner_samples, 0)
    hear(1)
    spread(2)

    for side, there in ((0, has_left), (1, has_right)):

        @pl.when(there)
        def _():
            for copy in halo_copies(1 - side):
                copy.wait_recv()

        @pl.when(jnp.logical_not(there))
        def _():
            slab_in[side] = jnp.zeros((5, 16, DEPTH), BF16)
            rim_in[side] = jnp.zeros((16, DEPTH), BF16)

    for side in range(2):
        away = -ROWS if side == 0 else ROWS
        for k, (time, x) in enumerate(sent[1 - side]):
            both = slab_in[side, k].astype(F32)
            pbuf[time, HALO + x + away] = both[:SHOTS]
            qbuf[time, HALO + x + away] = both[SHOTS:]
        first = 1 if side == 0 else HALO + ROWS
        rim = rim_in[side].astype(F32)
        for k, number in enumerate(RIM):
            coef[number, pl.ds(first + 4, 3)] = rim[3 * k : 3 * k + 3]
        coef[1, pl.ds(first + 4, 3)] = 1.0 - rim[:3]
        turns_up, turns_down = shifted(rim[:8])
        rest_up, rest_down = shifted(1.0 - rim[:8])
        for number, value, start in (
            (6, turns_up, 0),
            (7, rest_up, 0),
            (8, turns_up, 3),
            (9, turns_down, 0),
            (10, rest_down, 0),
            (11, turns_down, 3),
        ):
            coef[number, pl.ds(first + 4, 3)] = value[start : start + 3]

    def outer_step(moment, carry):
        def group(side, carry):
            some_rows(moment, jnp.where(side == 0, moment, HALO + ROWS - moment), 4)
            return carry

        return lax.fori_loop(0, 2, group, carry)

    some_rows(1, HALO - 1, 2)
    some_rows(1, HALO + ROWS - 1, 2)
    lax.fori_loop(2, STEPS + 1, outer_step, 0)

    edges = jnp.concatenate(
        [
            pbuf[moment + 1, pl.ds(first + HALO, HALO)].reshape(HALO * SHOTS, DEPTH)
            for moment in range(1, STEPS + 1)
            for first in (0, ROWS - HALO)
        ],
        axis=0,
    )
    high, low = split(edges)
    values = jnp.dot(high, onehot[...], preferred_element_type=F32) + jnp.dot(
        low, onehot[...], preferred_element_type=F32
    )
    for moment in range(STEPS):
        total = samples[moment]
        for k in range(2 * HALO):
            x = k if k < HALO else ROWS - 2 * HALO + k
            start = (moment * 2 * HALO + k) * SHOTS
            total = total + jnp.where(target_x == x, values[start : start + SHOTS], 0.0)
        samples[moment] = total

    spectra_load.wait()

    def feat_copy(s):
        rows = pl.ds(pl.multiple_of(s * 32, 32), 32)
        return pltpu.make_async_remote_copy(
            src_ref=feats.at[core, rows],
            dst_ref=feats.at[core, rows],
            send_sem=feat_send.at[s],
            recv_sem=feat_recv.at[s],
            device_id=mate,
            device_id_type=MESH,
        )

    def transform(s, carry):
        drawn = [samples[moment, pl.ds(s, 1)] for moment in range(STEPS)]
        for t in range(TILES):
            lanes = pl.ds(128 * t, 128)
            value = spec[s, :, lanes]
            for moment in range(STEPS):
                value = value + table[moment] * drawn[moment][:, 128 * t : 128 * (t + 1)]
            spec[s, :, lanes] = value
            feats[core, pl.ds(s * 32, 32), lanes] = value.astype(BF16)
        feat_copy(s).start()
        return carry

    lax.fori_loop(0, SHOTS, transform, 0)

    def energy_of(which):
        rows = feats[which]
        return jnp.dot(
            jnp.ones((8, SHOTS * 32), BF16), rows * rows, preferred_element_type=F32
        )

    pairs = ((0, 0), (0, 1), (0, 2), (2, 2), (2, 3))

    def products_of(which):
        blocks = [
            feats[which, :, pl.ds(pl.multiple_of(lax.rem(core + k, 4) * 128, 128), 128)]
            for k in range(4)
        ]
        found = []
        for left, right in ((0, (0, 1, 2)), (2, (2, 3))):
            product = lax.dot_general(
                blocks[left],
                jnp.concatenate([blocks[k] for k in right], axis=1),
                (((0,), (0,)), ((), ())),
                preferred_element_type=F32,
            )
            found += [product[:, 128 * k : 128 * (k + 1)] for k in range(len(right))]
        return found

    own_energy = energy_of(core)
    for number, product in enumerate(products_of(core)):
        half[number] = product
    for s in range(SHOTS):
        feat_copy(s).wait_recv()

    energy[chip] = own_energy + energy_of(1 - core)

    def energy_copy(place, owner):
        return pltpu.make_async_remote_copy(
            src_ref=energy.at[owner, pl.ds(0, 1)],
            dst_ref=energy.at[owner, pl.ds(0, 1)],
            send_sem=energy_send.at[place],
            recv_sem=energy_recv.at[owner],
            device_id={"shot": 2 * place + core},
            device_id_type=MESH,
        )

    hear(2)
    for hop in FAR_FIRST:
        energy_copy(lax.rem(chip + hop, CHIPS), chip).start()

    def units(place):
        level = energy[place, pl.ds(0, 1)]
        inverse = jnp.where(level > 0.0, lax.rsqrt(level), 0.0)
        return level * inverse, inverse

    def in_order(row):
        straight = [row[:, 128 * k : 128 * (k + 1)] for k in range(4)]
        return [jnp.where(core == 0, straight[k], straight[(k + 1) % 4]) for k in range(4)]

    row_number = lax.broadcasted_iota(jnp.int32, (128, 128), 0)
    lane_number = lax.broadcasted_iota(jnp.int32, (128, 128), 1)

    def upright(row, first, count):
        here = lane_number[:count] == row_number[:count] + first
        return jnp.sum(jnp.where(here, row, 0.0), axis=1, keepdims=True)

    inverses = in_order(units(chip)[1])
    columns = {k: upright(inverses[k] * FULL, 0, 128) for k in (0, 2)}
    for number, product in enumerate(products_of(1 - core)):
        left, right = pairs[number]
        value = half[number] + product
        half[number] = value
        part_out[number] = jnp.round(value * columns[left] * (inverses[right] * FULL)).astype(
            jnp.int16
        )

    def rows_of(place):
        return pl.ds(pl.multiple_of(place * CHUNK, CHUNK), CHUNK)

    def part_copy(place, owner):
        return pltpu.make_async_remote_copy(
            src_ref=part_out.at[:, rows_of(place)],
            dst_ref=part_in.at[owner],
            send_sem=part_send.at[place],
            recv_sem=part_recv.at[owner],
            device_id={"shot": 2 * place + core},
            device_id_type=MESH,
        )

    for hop in FAR_FIRST:
        part_copy(lax.rem(chip + hop, CHIPS), chip).start()

    start = chip * CHUNK
    total = [half[k, rows_of(chip)] for k in range(5)]
    for hop in NEAR_FIRST:
        place = lax.rem(chip + hop, CHIPS)
        energy_copy(place, place).wait_recv()
        roots = in_order(units(place)[0])
        columns = {k: upright(roots[k] * (1.0 / FULL), start, CHUNK) for k in (0, 2)}
        part_copy(place, place).wait_recv()
        for k, (left, right) in enumerate(pairs):
            total[k] = total[k] + part_in[place, k].astype(F32) * columns[left] * (roots[right] * (1.0 / FULL))

    level = energy[0, pl.ds(0, 1)]
    for k in range(1, CHIPS):
        level = level + energy[k, pl.ds(0, 1)]
    inverse = jnp.where(level > 0.0, lax.rsqrt(level), 0.0)
    root = level * inverse
    inverses = in_order(inverse)
    columns = {k: upright(inverses[k] * FULL, start, CHUNK) for k in (0, 2)}
    for k, (left, right) in enumerate(pairs):
        gathered[core, k, rows_of(chip)] = jnp.round(
            total[k] * columns[left] * (inverses[right] * FULL)
        ).astype(jnp.int16)

    def ring_copy(owner, place):
        return pltpu.make_async_remote_copy(
            src_ref=gathered.at[core, :, rows_of(owner)],
            dst_ref=gathered.at[core, :, rows_of(owner)],
            send_sem=ring_send.at[place],
            recv_sem=ring_recv.at[owner],
            device_id={"shot": 2 * place + core},
            device_id_type=MESH,
        )

    def pass_copy(owner, which):
        return pltpu.make_async_remote_copy(
            src_ref=gathered.at[which, :, rows_of(owner)],
            dst_ref=gathered.at[which, :, rows_of(owner)],
            send_sem=pass_send.at[owner],
            recv_sem=pass_recv.at[owner],
            device_id=mate,
            device_id_type=MESH,
        )

    for hop in FAR_FIRST:
        ring_copy(chip, lax.rem(chip + hop, CHIPS)).start()
    pass_copy(chip, core).start()

    for hop in NEAR_FIRST:
        place = lax.rem(chip + hop, CHIPS)
        ring_copy(place, place).wait_recv()
        pass_copy(place, core).start()
    def strips_of(which):
        grid = [gathered[which, k].astype(F32) for k in range(5)]

        def picks(first, count):
            return [
                chosen[pl.ds(pl.multiple_of(lax.rem(which + k, 4) * 128, 128), 128)]
                for k in range(first, first + count)
            ]

        for row, left, right in (
            (0, [0.5 * grid[0], grid[1], grid[2]], picks(0, 3)),
            (2, [0.5 * grid[3], grid[4]], picks(2, 2)),
        ):
            high, low = split(jnp.concatenate(left, axis=1))
            right = jnp.concatenate(right, axis=0)
            strips[which + row] = jnp.dot(high, right, preferred_element_type=F32) + jnp.dot(
                low, right, preferred_element_type=F32
            )

    strips_of(core)
    for hop in (0,) + NEAR_FIRST:
        pass_copy(lax.rem(chip + hop, CHIPS), 1 - core).wait_recv()
    strips_of(1 - core)
    strip_high, strip_low = split(strips[...].reshape(512, P_MAX * PATCH))
    root_high, root_low = split(jnp.broadcast_to(root * (1.0 / FULL), (8, DEPTH)))
    chosen_root = jnp.dot(root_high, chosen[...], preferred_element_type=F32) + jnp.dot(
        root_low, chosen[...], preferred_element_type=F32
    )
    for p in range(P_MAX):
        lanes = slice(PATCH * p, PATCH * (p + 1))
        dims = (((0,), (0,)), ((), ()))
        tile = lax.dot_general(
            chosen[:, lanes], strip_high[:, lanes], dims, preferred_element_type=F32
        ) + lax.dot_general(
            chosen[:, lanes], strip_low[:, lanes], dims, preferred_element_type=F32
        )
        live = (counts_ref[0, 0] > p).astype(F32) * (1.0 / (2 * CHIPS * SHOTS * 32))
        scale = chosen_root[0:1, lanes]
        gram_ref[p] = ((tile + tile.T) * scale).T * (scale * live)

    for side, there in ((0, has_left), (1, has_right)):

        @pl.when(there)
        def _():
            for copy in halo_copies(side):
                copy.wait_send()

    for s in range(SHOTS):
        feat_copy(s).wait_send()
    for hop in FAR_FIRST:
        place = lax.rem(chip + hop, CHIPS)
        energy_copy(place, chip).wait_send()
        part_copy(place, chip).wait_send()
        ring_copy(chip, place).wait_send()
    for hop in (0,) + NEAR_FIRST:
        pass_copy(lax.rem(chip + hop, CHIPS), core).wait_send()


def deliver(pbuf, qbuf, spec, gram, p_out, q_out, spectra_out, gram_out, sem):
    copies = [
        pltpu.make_async_copy(spec, spectra_out, sem.at[2]),
        pltpu.make_async_copy(gram, gram_out, sem.at[3]),
    ]
    for number, (source, target) in enumerate(((pbuf, p_out), (qbuf, q_out))):
        for s in range(SHOTS):
            copies.append(
                pltpu.make_async_copy(
                    source.at[STEPS + 1, pl.ds(HALO, ROWS), s], target.at[s], sem.at[number]
                )
            )
    for copy in copies:
        copy.start()
    for copy in copies:
        copy.wait()


def shards(
    bricks,
    pressure,
    auxiliary,
    pressure_prior,
    auxiliary_prior,
    courant_sq,
    thomsen_epsilon,
    thomsen_delta,
    tilt_angle,
    frequencies,
    spectra,
    target_cells,
    patch_lists,
    patch_counts,
):
    vmem = pl.BlockSpec(memory_space=pltpu.VMEM)
    whole = pl.BlockSpec(memory_space=pltpu.HBM)
    history = pltpu.VMEM((STEPS + 2, ROWS + 2 * HALO, SHOTS, DEPTH), F32)
    dma = pltpu.SemaphoreType.DMA
    made = pl.pallas_call(
        functools.partial(kernel, bricks),
        out_shape=(
            history,
            history,
            pltpu.VMEM((SHOTS, 32, DEPTH), F32),
            pltpu.VMEM((P_MAX, PATCH, PATCH), F32),
        ),
        in_specs=[whole] * 13,
        out_specs=(vmem,) * 4,
        scratch_shapes=[
            pltpu.SMEM((16,), F32),
            pltpu.SMEM((1, 1), jnp.int32),
            pltpu.VMEM((1, DEPTH), jnp.int32),
            pltpu.VMEM((P_MAX, 2 * CHIPS, PATCH), jnp.int32),
            pltpu.VMEM((4, ROWS, DEPTH), F32),
            pltpu.VMEM((12, ROWS + 16, DEPTH), F32),
            pltpu.VMEM((2, 5, 16, DEPTH), BF16),
            pltpu.VMEM((2, 5, 16, DEPTH), BF16),
            pltpu.VMEM((2, 16, DEPTH), BF16),
            pltpu.VMEM((2, 16, DEPTH), BF16),
            pltpu.VMEM((DEPTH, DEPTH), BF16),
            pltpu.VMEM((512, P_MAX * PATCH), BF16),
            pltpu.VMEM((STEPS, 32, 128), F32),
            pltpu.VMEM((STEPS, SHOTS, DEPTH), F32),
            pltpu.VMEM((2, SHOTS * 32, DEPTH), BF16),
            pltpu.VMEM((CHIPS, 8, DEPTH), F32),
            pltpu.VMEM((5, 128, 128), F32),
            pltpu.VMEM((5, 128, 128), jnp.int16),
            pltpu.VMEM((CHIPS, 5, CHUNK, 128), jnp.int16),
            pltpu.VMEM((2, 5, 128, 128), jnp.int16),
            pltpu.VMEM((4, 128, P_MAX * PATCH), F32),
            pltpu.SemaphoreType.REGULAR((3, 2)),
            dma((10,)),
            dma((2, 2)),
            dma((2, 2)),
            dma((SHOTS,)),
            dma((SHOTS,)),
            dma((CHIPS,)),
            dma((CHIPS,)),
            dma((CHIPS,)),
            dma((CHIPS,)),
            dma((CHIPS,)),
            dma((CHIPS,)),
            dma((CHIPS,)),
            dma((CHIPS,)),
        ],
        compiler_params=pltpu.CompilerParams(
            collective_id=0, has_side_effects=True, vmem_limit_bytes=50 << 20
        ),
    )(
        frequencies,
        patch_counts,
        courant_sq,
        thomsen_epsilon,
        thomsen_delta,
        tilt_angle,
        target_cells.reshape(1, -1),
        jnp.transpose(patch_lists[0], (1, 0, 2)),
        pressure,
        auxiliary,
        pressure_prior,
        auxiliary_prior,
        spectra,
    )
    field = jax.ShapeDtypeStruct((SHOTS, ROWS, DEPTH), F32)
    p_out, q_out, spectra_out, gram = pl.pallas_call(
        deliver,
        out_shape=(field, field, field, jax.ShapeDtypeStruct((P_MAX, PATCH, PATCH), F32)),
        in_specs=[vmem] * 4,
        out_specs=(whole,) * 4,
        scratch_shapes=[dma((4,))],
        compiler_params=pltpu.CompilerParams(vmem_limit_bytes=8 << 20),
    )(*(pltpu.with_memory_space_constraint(array, pltpu.VMEM) for array in made))
    return p_out, q_out, spectra_out, gram.reshape(1, 1, P_MAX, PATCH, PATCH)


def solution(mesh):
    return jax.shard_map(
        functools.partial(shards, mesh.shape["brick"]),
        mesh=mesh,
        in_specs=(
            P("shot", "brick", None),
            P("shot", "brick", None),
            P("shot", "brick", None),
            P("shot", "brick", None),
            P("brick", None),
            P("brick", None),
            P("brick", None),
            P("brick", None),
            P(),
            P("shot", None, "brick"),
            P("brick"),
            P("brick", None, None, None),
            P("brick", "shot"),
        ),
        out_specs=(
            P("shot", "brick", None),
            P("shot", "brick", None),
            P("shot", None, "brick"),
            P("brick", "shot", None, None, None),
        ),
        check_vma=False,
    )
```

```python
import functools

import jax
import jax.numpy as jnp
from jax import lax
from jax.experimental import pallas as pl
from jax.experimental.pallas import tpu as pltpu
from jax.sharding import PartitionSpec as P

STEPS = 4
PATCH = 128
P_MAX = 3
SHOTS = 8
ROWS = 32
HALO = 4
DEPTH = 512
TILES = DEPTH // 128
CHIPS = 8
CHUNK = 128 // CHIPS
RIM = (0, 2, 3, 4, 5)
FULL = 178.0
MESH = pl.DeviceIdType.MESH
F32 = jnp.float32
BF16 = jnp.bfloat16

FAR_FIRST = (4, 3, 5, 2, 6, 1, 7)
NEAR_FIRST = (1, 7, 2, 6, 3, 5, 4)


def split(value):
    high = value.astype(BF16)
    return high, (value - high.astype(F32)).astype(BF16)


def kernel(
    bricks,
    freq_in,
    counts_in,
    courant_in,
    epsilon_in,
    delta_in,
    tilt_in,
    cells_in,
    lists_in,
    p_in,
    q_in,
    pp_in,
    qq_in,
    spectra_in,
    pbuf,
    qbuf,
    spec,
    gram_ref,
    freq_ref,
    counts_ref,
    cells_ref,
    lists_ref,
    model,
    coef,
    slab_out,
    slab_in,
    rim_out,
    rim_in,
    onehot,
    chosen,
    table,
    samples,
    feats,
    energy,
    half,
    part_out,
    part_in,
    gathered,
    strips,
    word,
    in_sem,
    halo_send,
    halo_recv,
    feat_send,
    feat_recv,
    energy_send,
    energy_recv,
    part_send,
    part_recv,
    ring_send,
    ring_recv,
    pass_send,
    pass_recv,
):
    shot = lax.axis_index("shot")
    brick = lax.axis_index("brick")
    chip = shot // 2
    core = lax.rem(shot, 2)
    has_left = brick > 0
    has_right = brick < bricks - 1

    barrier = pltpu.get_barrier_semaphore()
    mate = {"shot": 2 * chip + 1 - core}
    chip_up = {"shot": 2 * lax.rem(chip + 1, CHIPS) + core}
    chip_down = {"shot": 2 * lax.rem(chip + CHIPS - 1, CHIPS) + core}
    for other in (mate, chip_up, chip_down):
        pl.semaphore_signal(barrier, inc=1, device_id=other, device_id_type=MESH)

    @pl.when(has_left)
    def _():
        pl.semaphore_signal(barrier, inc=1, device_id={"brick": brick - 1}, device_id_type=MESH)

    @pl.when(has_right)
    def _():
        pl.semaphore_signal(barrier, inc=1, device_id={"brick": brick + 1}, device_id_type=MESH)

    model_loads = [
        pltpu.make_async_copy(source, model.at[k], in_sem.at[5])
        for k, source in enumerate((courant_in, epsilon_in, delta_in, tilt_in))
    ]
    for load in model_loads:
        load.start()
    loads = []
    for number, (source, target, slot) in enumerate(
        ((p_in, pbuf, 1), (q_in, qbuf, 1), (pp_in, pbuf, 0), (qq_in, qbuf, 0))
    ):
        for s in range(SHOTS):
            loads.append(
                pltpu.make_async_copy(
                    source.at[s],
                    target.at[slot, pl.ds(HALO, ROWS), s],
                    in_sem.at[number],
                )
            )
    for load in loads:
        load.start()
    spectra_load = pltpu.make_async_copy(spectra_in, spec, in_sem.at[4])
    spectra_load.start()
    small_loads = [
        pltpu.make_async_copy(source, target, in_sem.at[6 + k])
        for k, (source, target) in enumerate(
            (
                (freq_in, freq_ref),
                (counts_in, counts_ref),
                (cells_in, cells_ref),
                (lists_in, lists_ref),
            )
        )
    ]
    for load in small_loads:
        load.start()

    def shifted(value):
        lane = lax.broadcasted_iota(jnp.int32, value.shape, 1)
        return (
            jnp.where(lane == 0, 0.0, pltpu.roll(value, 1, 1)),
            jnp.where(lane == DEPTH - 1, 0.0, pltpu.roll(value, DEPTH - 1, 1)),
        )

    for load in model_loads:
        load.wait()
    sine = jnp.sin(model[3])
    cosine = jnp.cos(model[3])
    courant = model[0]
    own = pl.ds(8, ROWS)
    turns = (cosine * cosine, sine * sine, 0.5 * sine * cosine)
    for k, value in enumerate(turns):
        coef[k, own] = value
        coef[6 + k, own], coef[9 + k, own] = shifted(value)
    coef[3, own] = courant
    coef[4, own] = courant * (1.0 + 2.0 * model[1])
    coef[5, own] = courant * (1.0 + 2.0 * model[2])
    for side, first in ((0, 8), (1, 8 + ROWS - 3)):
        rim_out[side] = jnp.concatenate(
            [coef[k, pl.ds(first, 3)] for k in RIM] + [jnp.zeros((1, DEPTH), F32)], axis=0
        ).astype(BF16)
    for load in loads:
        load.wait()
    lane = lax.broadcasted_iota(jnp.int32, (SHOTS, 128), 1)
    first_lane = lane == 0
    last_lane = lane == 127

    def tiles(value):
        return [value[:, 128 * k : 128 * (k + 1)] for k in range(TILES)]

    def deeper(value):
        turned = [pltpu.roll(tile, 127, 1) for tile in value]
        return [jnp.where(last_lane, turned[(k + 1) % TILES], turned[k]) for k in range(TILES)]

    def shallower(value):
        turned = [pltpu.roll(tile, 1, 1) for tile in value]
        return [jnp.where(first_lane, turned[k - 1], turned[k]) for k in range(TILES)]

    def mix(first, a, second, b, sign):
        if sign > 0:
            return [w * x + v * y for w, x, v, y in zip(first, a, second, b)]
        return [w * x - v * y for w, x, v, y in zip(first, a, second, b)]

    def some_rows(moment, row, count):
        p_rows = [tiles(pbuf[moment, row + k]) for k in range(-1, count + 1)]
        q_rows = [tiles(qbuf[moment, row + k]) for k in range(-1, count + 1)]
        for k in range(count):
            at = row + k
            (
                cos_sq,
                sin_sq,
                speed,
                speed_e,
                speed_d,
                cos_up,
                sin_up,
                twist_up,
                cos_down,
                sin_down,
                twist_down,
            ) = (
                tiles(jnp.broadcast_to(coef[number, pl.ds(at + 4, 1)], (SHOTS, DEPTH)))
                for number in (0, 1, 3, 4, 5, 6, 7, 8, 9, 10, 11)
            )
            p_steep = [a + b for a, b in zip(p_rows[k], p_rows[k + 2])]
            p_slope = [b - a for a, b in zip(p_rows[k], p_rows[k + 2])]
            q_steep = [a + b for a, b in zip(q_rows[k], q_rows[k + 2])]
            q_slope = [b - a for a, b in zip(q_rows[k], q_rows[k + 2])]
            p_deeper = deeper(mix(sin_up, p_rows[k + 1], twist_up, p_slope, -1))
            p_shallower = shallower(mix(sin_down, p_rows[k + 1], twist_down, p_slope, 1))
            q_deeper = deeper(mix(cos_up, q_rows[k + 1], twist_up, q_slope, 1))
            q_shallower = shallower(mix(cos_down, q_rows[k + 1], twist_down, q_slope, -1))
            p_old = tiles(pbuf[moment - 1, at])
            q_old = tiles(qbuf[moment - 1, at])
            for t in range(TILES):
                p_two = p_rows[k + 1][t] + p_rows[k + 1][t]
                q_two = q_rows[k + 1][t] + q_rows[k + 1][t]
                across = (cos_sq[t] * p_steep[t] - p_two) + (p_deeper[t] + p_shallower[t])
                along = (sin_sq[t] * q_steep[t] - q_two) + (q_deeper[t] + q_shallower[t])
                push = speed[t] * along
                lanes = pl.ds(128 * t, 128)
                pbuf[moment + 1, at, :, lanes] = (p_two - p_old[t]) + (speed_e[t] * across + push)
                qbuf[moment + 1, at, :, lanes] = (q_two - q_old[t]) + (speed_d[t] * across + push)

    some_rows(1, HALO + 1, 2)
    some_rows(1, HALO + ROWS - 3, 2)

    sent = (((1, 0), (1, 1), (0, 0), (2, 1), (2, 2)), ((1, 31), (1, 30), (0, 31), (2, 30), (2, 29)))
    for side in range(2):
        for k, (time, x) in enumerate(sent[side]):
            slab_out[side, k] = jnp.concatenate(
                [pbuf[time, HALO + x], qbuf[time, HALO + x]], axis=0
            ).astype(BF16)

    pl.semaphore_wait(
        barrier, 3 + has_left.astype(jnp.int32) + has_right.astype(jnp.int32)
    )

    def spread(j):
        pl.semaphore_signal(word.at[j, 0], inc=1, device_id=chip_up, device_id_type=MESH)
        pl.semaphore_signal(word.at[j, 1], inc=1, device_id=chip_down, device_id_type=MESH)

    def hear(j):
        pl.semaphore_wait(word.at[j, 0], 1)
        pl.semaphore_wait(word.at[j, 1], 1)

    spread(0)

    def halo_copies(side):
        target = {"brick": brick - 1 if side == 0 else brick + 1}
        return [
            pltpu.make_async_remote_copy(
                src_ref=slab_out.at[side],
                dst_ref=slab_in.at[1 - side],
                send_sem=halo_send.at[side, 0],
                recv_sem=halo_recv.at[1 - side, 0],
                device_id=target,
                device_id_type=MESH,
            ),
            pltpu.make_async_remote_copy(
                src_ref=rim_out.at[side],
                dst_ref=rim_in.at[1 - side],
                send_sem=halo_send.at[side, 1],
                recv_sem=halo_recv.at[1 - side, 1],
                device_id=target,
                device_id_type=MESH,
            ),
        ]

    for side, there in ((0, has_left), (1, has_right)):

        @pl.when(there)
        def _():
            for copy in halo_copies(side):
                copy.start()

    for load in small_loads:
        load.wait()
    cells = cells_ref[...]
    target_x = cells >> 9
    target_z = cells & (DEPTH - 1)
    onehot[...] = (
        lax.broadcasted_iota(jnp.int32, (DEPTH, DEPTH), 0) == target_z
    ).astype(F32).astype(BF16)

    for p in range(P_MAX):
        chosen[:, pl.ds(PATCH * p, PATCH)] = (
            (lax.broadcasted_iota(jnp.int32, (512, PATCH), 0) == lists_ref[p, pl.ds(shot, 1)])
            .astype(F32)
            .astype(BF16)
        )

    number = lax.broadcasted_iota(jnp.int32, (16, 128), 0)
    frequency = jnp.zeros((16, 128), F32)
    for k in range(16):
        frequency = jnp.where(number == k, freq_ref[k], frequency)
    for moment in range(STEPS):
        angle = frequency * (moment + 1.0)
        table[moment, pl.ds(0, 16)] = jnp.cos(angle)
        table[moment, pl.ds(16, 16)] = -jnp.sin(angle)

    def inner_step(moment, carry):
        def group(number, carry):
            some_rows(moment, moment + HALO + 4 * number, 4)
            return carry

        return lax.fori_loop(0, (ROWS - 2 * moment + 3) // 4, group, carry)

    lax.fori_loop(1, STEPS + 1, inner_step, 0)
    hear(0)
    spread(1)

    def picked(moment, first, count):
        rows = pbuf[moment + 1, pl.ds(first + HALO, count)].reshape(count * SHOTS, DEPTH)
        high, low = split(rows)
        values = jnp.dot(high, onehot[...], preferred_element_type=F32) + jnp.dot(
            low, onehot[...], preferred_element_type=F32
        )
        total = jnp.zeros((SHOTS, DEPTH), F32)
        for k in range(count):
            total = total + jnp.where(
                target_x == first + k, values[k * SHOTS : (k + 1) * SHOTS], 0.0
            )
        return total

    def inner_samples(moment, carry):
        samples[moment - 1] = picked(moment, HALO, ROWS - 2 * HALO)
        return carry

    lax.fori_loop(1, STEPS + 1, inner_samples, 0)
    hear(1)
    spread(2)

    for side, there in ((0, has_left), (1, has_right)):

        @pl.when(there)
        def _():
            for copy in halo_copies(1 - side):
                copy.wait_recv()

        @pl.when(jnp.logical_not(there))
        def _():
            slab_in[side] = jnp.zeros((5, 16, DEPTH), BF16)
            rim_in[side] = jnp.zeros((16, DEPTH), BF16)

    for side in range(2):
        away = -ROWS if side == 0 else ROWS
        for k, (time, x) in enumerate(sent[1 - side]):
            both = slab_in[side, k].astype(F32)
            pbuf[time, HALO + x + away] = both[:SHOTS]
            qbuf[time, HALO + x + away] = both[SHOTS:]
        first = 1 if side == 0 else HALO + ROWS
        rim = rim_in[side].astype(F32)
        for k, number in enumerate(RIM):
            coef[number, pl.ds(first + 4, 3)] = rim[3 * k : 3 * k + 3]
        coef[1, pl.ds(first + 4, 3)] = 1.0 - rim[:3]
        turns_up, turns_down = shifted(rim[:8])
        rest_up, rest_down = shifted(1.0 - rim[:8])
        for number, value, start in (
            (6, turns_up, 0),
            (7, rest_up, 0),
            (8, turns_up, 3),
            (9, turns_down, 0),
            (10, rest_down, 0),
            (11, turns_down, 3),
        ):
            coef[number, pl.ds(first + 4, 3)] = value[start : start + 3]

    def outer_step(moment, carry):
        some_rows(moment, moment, 4)
        some_rows(moment, HALO + ROWS - moment, 4)
        return carry

    some_rows(1, HALO - 1, 2)
    some_rows(1, HALO + ROWS - 1, 2)
    lax.fori_loop(2, STEPS + 1, outer_step, 0)

    edges = jnp.concatenate(
        [
            pbuf[moment + 1, pl.ds(first + HALO, HALO)].reshape(HALO * SHOTS, DEPTH)
            for moment in range(1, STEPS + 1)
            for first in (0, ROWS - HALO)
        ],
        axis=0,
    )
    high, low = split(edges)
    values = jnp.dot(high, onehot[...], preferred_element_type=F32) + jnp.dot(
        low, onehot[...], preferred_element_type=F32
    )
    for moment in range(STEPS):
        total = samples[moment]
        for k in range(2 * HALO):
            x = k if k < HALO else ROWS - 2 * HALO + k
            start = (moment * 2 * HALO + k) * SHOTS
            total = total + jnp.where(target_x == x, values[start : start + SHOTS], 0.0)
        samples[moment] = total

    spectra_load.wait()

    def feat_copy(s):
        rows = pl.ds(pl.multiple_of(s * 32, 32), 32)
        return pltpu.make_async_remote_copy(
            src_ref=feats.at[core, rows],
            dst_ref=feats.at[core, rows],
            send_sem=feat_send.at[s],
            recv_sem=feat_recv.at[s],
            device_id=mate,
            device_id_type=MESH,
        )

    def transform(s, carry):
        drawn = [samples[moment, pl.ds(s, 1)] for moment in range(STEPS)]
        for t in range(TILES):
            lanes = pl.ds(128 * t, 128)
            value = spec[s, :, lanes]
            for moment in range(STEPS):
                value = value + table[moment] * drawn[moment][:, 128 * t : 128 * (t + 1)]
            spec[s, :, lanes] = value
            feats[core, pl.ds(s * 32, 32), lanes] = value.astype(BF16)
        feat_copy(s).start()
        return carry

    lax.fori_loop(0, SHOTS, transform, 0)

    def energy_of(which):
        rows = feats[which]
        return jnp.dot(
            jnp.ones((8, SHOTS * 32), BF16), rows * rows, preferred_element_type=F32
        )

    pairs = ((0, 0), (0, 1), (0, 2), (2, 2), (2, 3))

    def products_of(which):
        blocks = [
            feats[which, :, pl.ds(pl.multiple_of(lax.rem(core + k, 4) * 128, 128), 128)]
            for k in range(4)
        ]
        found = []
        for left, right in ((0, (0, 1, 2)), (2, (2, 3))):
            product = lax.dot_general(
                blocks[left],
                jnp.concatenate([blocks[k] for k in right], axis=1),
                (((0,), (0,)), ((), ())),
                preferred_element_type=F32,
            )
            found += [product[:, 128 * k : 128 * (k + 1)] for k in range(len(right))]
        return found

    own_energy = energy_of(core)
    for number, product in enumerate(products_of(core)):
        half[number] = product
    for s in range(SHOTS):
        feat_copy(s).wait_recv()

    energy[chip] = own_energy + energy_of(1 - core)

    def energy_copy(place, owner):
        return pltpu.make_async_remote_copy(
            src_ref=energy.at[owner, pl.ds(0, 1)],
            dst_ref=energy.at[owner, pl.ds(0, 1)],
            send_sem=energy_send.at[place],
            recv_sem=energy_recv.at[owner],
            device_id={"shot": 2 * place + core},
            device_id_type=MESH,
        )

    hear(2)
    for hop in FAR_FIRST:
        energy_copy(lax.rem(chip + hop, CHIPS), chip).start()

    def units(place):
        level = energy[place, pl.ds(0, 1)]
        inverse = jnp.where(level > 0.0, lax.rsqrt(level), 0.0)
        return level * inverse, inverse

    def in_order(row):
        straight = [row[:, 128 * k : 128 * (k + 1)] for k in range(4)]
        return [jnp.where(core == 0, straight[k], straight[(k + 1) % 4]) for k in range(4)]

    row_number = lax.broadcasted_iota(jnp.int32, (128, 128), 0)
    lane_number = lax.broadcasted_iota(jnp.int32, (128, 128), 1)

    def upright(row, first, count):
        here = lane_number[:count] == row_number[:count] + first
        return jnp.sum(jnp.where(here, row, 0.0), axis=1, keepdims=True)

    inverses = in_order(units(chip)[1])
    columns = {k: upright(inverses[k] * FULL, 0, 128) for k in (0, 2)}
    for number, product in enumerate(products_of(1 - core)):
        left, right = pairs[number]
        value = half[number] + product
        half[number] = value
        part_out[number] = jnp.round(value * columns[left] * (inverses[right] * FULL)).astype(
            jnp.int16
        )

    def rows_of(place):
        return pl.ds(pl.multiple_of(place * CHUNK, CHUNK), CHUNK)

    def part_copy(place, owner):
        return pltpu.make_async_remote_copy(
            src_ref=part_out.at[:, rows_of(place)],
            dst_ref=part_in.at[owner],
            send_sem=part_send.at[place],
            recv_sem=part_recv.at[owner],
            device_id={"shot": 2 * place + core},
            device_id_type=MESH,
        )

    for hop in FAR_FIRST:
        part_copy(lax.rem(chip + hop, CHIPS), chip).start()

    start = chip * CHUNK
    total = [half[k, rows_of(chip)] for k in range(5)]
    for hop in NEAR_FIRST:
        place = lax.rem(chip + hop, CHIPS)
        energy_copy(place, place).wait_recv()
        roots = in_order(units(place)[0])
        columns = {k: upright(roots[k] * (1.0 / FULL), start, CHUNK) for k in (0, 2)}
        part_copy(place, place).wait_recv()
        for k, (left, right) in enumerate(pairs):
            total[k] = total[k] + part_in[place, k].astype(F32) * columns[left] * (roots[right] * (1.0 / FULL))

    level = energy[0, pl.ds(0, 1)]
    for k in range(1, CHIPS):
        level = level + energy[k, pl.ds(0, 1)]
    inverse = jnp.where(level > 0.0, lax.rsqrt(level), 0.0)
    root = level * inverse
    inverses = in_order(inverse)
    columns = {k: upright(inverses[k] * FULL, start, CHUNK) for k in (0, 2)}
    for k, (left, right) in enumerate(pairs):
        gathered[core, k, rows_of(chip)] = jnp.round(
            total[k] * columns[left] * (inverses[right] * FULL)
        ).astype(jnp.int16)

    def ring_copy(owner, place):
        return pltpu.make_async_remote_copy(
            src_ref=gathered.at[core, :, rows_of(owner)],
            dst_ref=gathered.at[core, :, rows_of(owner)],
            send_sem=ring_send.at[place],
            recv_sem=ring_recv.at[owner],
            device_id={"shot": 2 * place + core},
            device_id_type=MESH,
        )

    def pass_copy(owner, which):
        return pltpu.make_async_remote_copy(
            src_ref=gathered.at[which, :, rows_of(owner)],
            dst_ref=gathered.at[which, :, rows_of(owner)],
            send_sem=pass_send.at[owner],
            recv_sem=pass_recv.at[owner],
            device_id=mate,
            device_id_type=MESH,
        )

    for hop in FAR_FIRST:
        ring_copy(chip, lax.rem(chip + hop, CHIPS)).start()
    pass_copy(chip, core).start()

    for hop in NEAR_FIRST:
        place = lax.rem(chip + hop, CHIPS)
        ring_copy(place, place).wait_recv()
        pass_copy(place, core).start()
    def strips_of(which):
        grid = [gathered[which, k].astype(F32) for k in range(5)]

        def picks(first, count):
            return [
                chosen[pl.ds(pl.multiple_of(lax.rem(which + k, 4) * 128, 128), 128)]
                for k in range(first, first + count)
            ]

        for row, left, right in (
            (0, [0.5 * grid[0], grid[1], grid[2]], picks(0, 3)),
            (2, [0.5 * grid[3], grid[4]], picks(2, 2)),
        ):
            high, low = split(jnp.concatenate(left, axis=1))
            right = jnp.concatenate(right, axis=0)
            strips[which + row] = jnp.dot(high, right, preferred_element_type=F32) + jnp.dot(
                low, right, preferred_element_type=F32
            )

    strips_of(core)
    for hop in (0,) + NEAR_FIRST:
        pass_copy(lax.rem(chip + hop, CHIPS), 1 - core).wait_recv()
    strips_of(1 - core)
    strip_high, strip_low = split(strips[...].reshape(512, P_MAX * PATCH))
    root_high, root_low = split(jnp.broadcast_to(root * (1.0 / FULL), (8, DEPTH)))
    chosen_root = jnp.dot(root_high, chosen[...], preferred_element_type=F32) + jnp.dot(
        root_low, chosen[...], preferred_element_type=F32
    )
    for p in range(P_MAX):
        lanes = slice(PATCH * p, PATCH * (p + 1))
        dims = (((0,), (0,)), ((), ()))
        tile = lax.dot_general(
            chosen[:, lanes], strip_high[:, lanes], dims, preferred_element_type=F32
        ) + lax.dot_general(
            chosen[:, lanes], strip_low[:, lanes], dims, preferred_element_type=F32
        )
        live = (counts_ref[0, 0] > p).astype(F32) * (1.0 / (2 * CHIPS * SHOTS * 32))
        scale = chosen_root[0:1, lanes]
        gram_ref[p] = ((tile + tile.T) * scale).T * (scale * live)

    for side, there in ((0, has_left), (1, has_right)):

        @pl.when(there)
        def _():
            for copy in halo_copies(side):
                copy.wait_send()

    for s in range(SHOTS):
        feat_copy(s).wait_send()
    for hop in FAR_FIRST:
        place = lax.rem(chip + hop, CHIPS)
        energy_copy(place, chip).wait_send()
        part_copy(place, chip).wait_send()
        ring_copy(chip, place).wait_send()
    for hop in (0,) + NEAR_FIRST:
        pass_copy(lax.rem(chip + hop, CHIPS), core).wait_send()


def deliver(pbuf, qbuf, spec, gram, p_out, q_out, spectra_out, gram_out, sem):
    copies = [
        pltpu.make_async_copy(spec, spectra_out, sem.at[2]),
        pltpu.make_async_copy(gram, gram_out, sem.at[3]),
    ]
    for number, (source, target) in enumerate(((pbuf, p_out), (qbuf, q_out))):
        for s in range(SHOTS):
            copies.append(
                pltpu.make_async_copy(
                    source.at[STEPS + 1, pl.ds(HALO, ROWS), s], target.at[s], sem.at[number]
                )
            )
    for copy in copies:
        copy.start()
    for copy in copies:
        copy.wait()


def shards(
    bricks,
    pressure,
    auxiliary,
    pressure_prior,
    auxiliary_prior,
    courant_sq,
    thomsen_epsilon,
    thomsen_delta,
    tilt_angle,
    frequencies,
    spectra,
    target_cells,
    patch_lists,
    patch_counts,
):
    vmem = pl.BlockSpec(memory_space=pltpu.VMEM)
    whole = pl.BlockSpec(memory_space=pltpu.HBM)
    history = pltpu.VMEM((STEPS + 2, ROWS + 2 * HALO, SHOTS, DEPTH), F32)
    dma = pltpu.SemaphoreType.DMA
    made = pl.pallas_call(
        functools.partial(kernel, bricks),
        out_shape=(
            history,
            history,
            pltpu.VMEM((SHOTS, 32, DEPTH), F32),
            pltpu.VMEM((P_MAX, PATCH, PATCH), F32),
        ),
        in_specs=[whole] * 13,
        out_specs=(vmem,) * 4,
        scratch_shapes=[
            pltpu.SMEM((16,), F32),
            pltpu.SMEM((1, 1), jnp.int32),
            pltpu.VMEM((1, DEPTH), jnp.int32),
            pltpu.VMEM((P_MAX, 2 * CHIPS, PATCH), jnp.int32),
            pltpu.VMEM((4, ROWS, DEPTH), F32),
            pltpu.VMEM((12, ROWS + 16, DEPTH), F32),
            pltpu.VMEM((2, 5, 16, DEPTH), BF16),
            pltpu.VMEM((2, 5, 16, DEPTH), BF16),
            pltpu.VMEM((2, 16, DEPTH), BF16),
            pltpu.VMEM((2, 16, DEPTH), BF16),
            pltpu.VMEM((DEPTH, DEPTH), BF16),
            pltpu.VMEM((512, P_MAX * PATCH), BF16),
            pltpu.VMEM((STEPS, 32, 128), F32),
            pltpu.VMEM((STEPS, SHOTS, DEPTH), F32),
            pltpu.VMEM((2, SHOTS * 32, DEPTH), BF16),
            pltpu.VMEM((CHIPS, 8, DEPTH), F32),
            pltpu.VMEM((5, 128, 128), F32),
            pltpu.VMEM((5, 128, 128), jnp.int16),
            pltpu.VMEM((CHIPS, 5, CHUNK, 128), jnp.int16),
            pltpu.VMEM((2, 5, 128, 128), jnp.int16),
            pltpu.VMEM((4, 128, P_MAX * PATCH), F32),
            pltpu.SemaphoreType.REGULAR((3, 2)),
            dma((10,)),
            dma((2, 2)),
            dma((2, 2)),
            dma((SHOTS,)),
            dma((SHOTS,)),
            dma((CHIPS,)),
            dma((CHIPS,)),
            dma((CHIPS,)),
            dma((CHIPS,)),
            dma((CHIPS,)),
            dma((CHIPS,)),
            dma((CHIPS,)),
            dma((CHIPS,)),
        ],
        compiler_params=pltpu.CompilerParams(
            collective_id=0, has_side_effects=True, vmem_limit_bytes=50 << 20
        ),
    )(
        frequencies,
        patch_counts,
        courant_sq,
        thomsen_epsilon,
        thomsen_delta,
        tilt_angle,
        target_cells.reshape(1, -1),
        jnp.transpose(patch_lists[0], (1, 0, 2)),
        pressure,
        auxiliary,
        pressure_prior,
        auxiliary_prior,
        spectra,
    )
    field = jax.ShapeDtypeStruct((SHOTS, ROWS, DEPTH), F32)
    p_out, q_out, spectra_out, gram = pl.pallas_call(
        deliver,
        out_shape=(field, field, field, jax.ShapeDtypeStruct((P_MAX, PATCH, PATCH), F32)),
        in_specs=[vmem] * 4,
        out_specs=(whole,) * 4,
        scratch_shapes=[dma((4,))],
        compiler_params=pltpu.CompilerParams(vmem_limit_bytes=8 << 20),
    )(*(pltpu.with_memory_space_constraint(array, pltpu.VMEM) for array in made))
    return p_out, q_out, spectra_out, gram.reshape(1, 1, P_MAX, PATCH, PATCH)


def solution(mesh):
    return jax.shard_map(
        functools.partial(shards, mesh.shape["brick"]),
        mesh=mesh,
        in_specs=(
            P("shot", "brick", None),
            P("shot", "brick", None),
            P("shot", "brick", None),
            P("shot", "brick", None),
            P("brick", None),
            P("brick", None),
            P("brick", None),
            P("brick", None),
            P(),
            P("shot", None, "brick"),
            P("brick"),
            P("brick", None, None, None),
            P("brick", "shot"),
        ),
        out_specs=(
            P("shot", "brick", None),
            P("shot", "brick", None),
            P("shot", None, "brick"),
            P("brick", "shot", None, None, None),
        ),
        check_vma=False,
    )
```
